128 devices in a mesh: tm: 4 (over x_hi, core), slope: 32 (over x_lo, z, y).
Axes of the slice: x: 4 (x_hi: 2, x_lo: 2; x = x_hi * 2 + x_lo), y: 4, z: 4, core: 2. Of those that a mesh axis runs over, the one named last changes fastest.
Arguments:
- telemetry: bfloat16 [32, 32, 96, 4096], P('slope', None, None, 'tm'), may hold values from -24 to 24
- frame_ids: int32 [4096], P('tm'), may hold values from 0 to 1023, as said below
- valid: int32 [8, 48], replicated, may hold values 0 or 1
- noise: float32 [1024], replicated, may hold values from 0.1 to 1
- prior_next: float32 [32, 32, 96, 1024], P('slope', 'tm'), may hold values from -2 to 2
Outputs:
- panel: float32 [32, 32, 96, 1024], P('slope', 'tm')
- next_block: float32 [32, 32, 96, 1024], P('slope', 'tm')
The draws below stay inside these ranges and needn't reach their ends.
Inputs may be any that keep to these rules, and one draw needn't show every extreme that they name: `frame_ids`: entry f names a frame of the block of 1024 buffer frames that starts at (f // 1024) * 1024; entries may repeat.
All inputs are finite; a program needn't handle non-finite values.
Results may differ from the reference program's by a relative error of at most 0.0003.
Values may be sent and summed in bfloat16 or wider, within the bound.
No kernel may reach another device: no remote copies, remote signals or barrier semaphores. Data moves between devices by JAX's collectives and lax.ppermute only.
A program may use at most 128 MiB of HBM per device.

```python
import math
import jax
import jax.numpy as jnp
from jax import lax

M = 98304
B = 1024
SENSORS = 8
SEGS = 48
FR_DEV = 1024
FRAMES = 4096
RB = 32
CYC = 96
N_SLOPE = 32


def draw_telemetry(key, part):
    keys = jax.random.split(key, 3)
    full_shape = (N_SLOPE, RB, CYC, FRAMES)
    noise_part = jax.random.truncated_normal(keys[0], -4.0, 4.0, full_shape)
    strength = 0.6
    amplitudes = jax.random.truncated_normal(keys[1], -3.0, 3.0, (2, FRAMES))
    loadings = jax.random.truncated_normal(keys[2], -3.0, 3.0, (2, N_SLOPE, RB, CYC, 1))
    common = loadings[0] * amplitudes[0] + loadings[1] * amplitudes[1]
    return (noise_part + strength * common).astype(jnp.bfloat16)


def draw_frame_ids(key, part):
    picks = jax.random.randint(key, (FRAMES,), 0, FR_DEV, dtype=jnp.int32)
    picks = picks.at[0].set(FR_DEV - 1)
    return picks.at[FRAMES - 1].set(0)


def touch_ends(drawn, rng, low, largest):
    spot = [jax.random.randint(jax.random.fold_in(rng, axis), (), 0, length) for axis, length in enumerate(drawn.shape)]
    longest = drawn.shape.index(max(drawn.shape))
    neighbour = spot[:longest] + [(spot[longest] + 1) % drawn.shape[longest]] + spot[longest + 1:]
    return drawn.at[tuple(spot)].set(low).at[tuple(neighbour)].set(largest)


def levels(key, dims, shards, smallest, top_value):
    level = 1.0
    for position, blocks in shards:
        draws = jax.random.uniform(jax.random.fold_in(jax.random.fold_in(key, 6), position), (blocks,), jnp.float32, smallest / len(shards), top_value / len(shards))
        level = level * jnp.repeat(jnp.exp(draws), dims[position] // blocks).reshape((-1,) + (1,) * (len(dims) - 1 - position))
    return level


def gaussian(rng, extent, deviation, reach, pieces=(), kind=jnp.bfloat16):
    factor_of = levels(rng, extent, pieces, -0.22, 0.18) if pieces else 1.0
    entries = jax.random.normal(rng, extent, jnp.float32) * deviation * factor_of
    return jnp.minimum(jnp.maximum(entries, -reach), reach).astype(kind)


def setup_inputs(seed: int = 0) -> dict:
    splits = jax.random.split(jax.random.key(seed), 6)
    return {
        "telemetry": draw_telemetry(jax.random.fold_in(splits[5], 71), 0),
        "frame_ids": draw_frame_ids(jax.random.fold_in(splits[5], 71), 0),
        "valid": touch_ends((jax.random.randint(splits[2], (SENSORS, SEGS), 0, 4) < 3).astype(jnp.int32), jax.random.fold_in(splits[2], 1), 0, 1),
        "noise": jnp.clip(jnp.exp(jax.random.uniform(splits[3], (B,), jnp.float32, math.log(0.1), math.log(1.0))), 0.1, 1.0),
        "prior_next": gaussian(splits[4], (N_SLOPE, RB, CYC, B), 0.3, 2.0, ((0, 32), (1, 4)), jnp.float32),
    }


def reference(telemetry, frame_ids, valid, noise, prior_next):
    positions = jnp.arange(FRAMES, dtype=jnp.int32)
    columns = positions // FR_DEV * FR_DEV + frame_ids.astype(jnp.int32)
    slope_ids = (jnp.arange(CYC, dtype=jnp.int32)[None, None, :] * N_SLOPE + jnp.arange(N_SLOPE, dtype=jnp.int32)[:, None, None]) * RB + jnp.arange(RB, dtype=jnp.int32)[None, :, None]
    per_sensor = M // SENSORS
    seg_len = per_sensor // SEGS
    keep_row = valid[slope_ids // per_sensor, slope_ids % per_sensor // seg_len].astype(jnp.bfloat16)

    def select_cycle(cycle_id):
        tel_cycle = lax.dynamic_index_in_dim(telemetry, cycle_id, 2, keepdims=False)
        mask_cycle = lax.dynamic_index_in_dim(keep_row, cycle_id, 2, keepdims=False)
        return jnp.take(tel_cycle, columns, axis=2) * mask_cycle[:, :, None]
    first_cols = select_cycle(0).reshape(B, FRAMES)

    def gram_cycle(cycle_id):
        row_slice = select_cycle(cycle_id).reshape(B, FRAMES)
        return jnp.dot(row_slice.astype(jnp.float32), first_cols.T.astype(jnp.float32), preferred_element_type=jnp.float32)
    stacked = lax.map(gram_cycle, jnp.arange(CYC, dtype=jnp.int32)) / FRAMES
    stacked = stacked.at[0].add(jnp.diag(noise))
    factor = jnp.linalg.cholesky(stacked[0])
    inverse = jax.scipy.linalg.solve_triangular(factor, jnp.eye(B, dtype=factor.dtype), lower=True)
    flat_block = stacked.reshape(CYC * B, B)
    panel_flat = jnp.dot(flat_block, inverse.T, precision=lax.Precision.HIGHEST)
    second = panel_flat[B:2 * B]
    update = jnp.dot(panel_flat, second.T, precision=lax.Precision.HIGHEST)
    panel = panel_flat.reshape(CYC, N_SLOPE, RB, B).transpose(1, 2, 0, 3)
    next_block = prior_next - update.reshape(CYC, N_SLOPE, RB, B).transpose(1, 2, 0, 3)
    return (panel, next_block)
```

```python
import jax
import jax.numpy as jnp
from jax import lax
from jax.experimental import pallas as pl
from jax.experimental.pallas import tpu as pltpu
from jax.sharding import PartitionSpec as P

NB = 128
MB = 8


def bf16_round(z):
    return z.astype(jnp.bfloat16).astype(jnp.float32)


def split3(z):
    high = bf16_round(z)
    rest = z - high
    mid = bf16_round(rest)
    return high, mid, rest - mid


def factor_block(wa, wx, out):
    sub = lax.broadcasted_iota(jnp.int32, (MB, NB), 0)
    for k in range(NB // MB):
        lo = MB * k
        a = wa[lo:lo + MB, :]
        x = wx[lo:lo + MB, :]
        cols = [jnp.broadcast_to(a[:, lo + j:lo + j + 1], (MB, NB)) for j in range(MB)]
        inv_d = jnp.zeros((MB, NB), jnp.float32)
        piv = jnp.zeros((MB, NB), jnp.float32)
        for j in range(MB):
            pivot = jnp.broadcast_to(cols[j][j:j + 1, :], (MB, NB))
            recip = 1.0 / pivot
            mult = jnp.where(sub > j, cols[j] * recip, 0.0)
            for l in range(j + 1, MB):
                cols[l] = cols[l] - mult * jnp.broadcast_to(cols[l][j:j + 1, :], (MB, NB))
            a = a - mult * jnp.broadcast_to(a[j:j + 1, :], (MB, NB))
            x = x - mult * jnp.broadcast_to(x[j:j + 1, :], (MB, NB))
            inv_d = jnp.where(sub == j, recip, inv_d)
            piv = jnp.where(sub == j, pivot, piv)
        out[lo:lo + MB, :] = x * (1.0 / jnp.sqrt(piv))
        if lo + MB == NB:
            break
        right = jnp.concatenate([a * inv_d, x * inv_d], axis=1)
        lh, lm, ll = split3(a)
        rh, rm, rl = split3(right)
        left_stack = jnp.concatenate([lh, lh, lm, lh, ll, lm], axis=0).astype(jnp.bfloat16)
        right_stack = jnp.concatenate([rh, rm, rh, rl, rh, rm], axis=0).astype(jnp.bfloat16)
        prod = lax.dot_general(left_stack, right_stack, (((0,), (0,)), ((), ())), preferred_element_type=jnp.float32)
        wa[lo + MB:, :] = wa[lo + MB:, :] - prod[lo + MB:, :NB]
        wx[lo + MB:, :] = wx[lo + MB:, :] - prod[lo + MB:, NB:]


def dot3(a, b, dims):
    ah = a.astype(jnp.bfloat16)
    al = (a - ah.astype(jnp.float32)).astype(jnp.bfloat16)
    bh = b.astype(jnp.bfloat16)
    bl = (b - bh.astype(jnp.float32)).astype(jnp.bfloat16)
    dot = lambda p, q: lax.dot_general(p, q, (dims, ((), ())), preferred_element_type=jnp.float32)
    return dot(ah, bh) + (dot(ah, bl) + dot(al, bh))


def chol_kernel(g_ref, o_ref, big, wa, wx, linv):
    n = g_ref.shape[0]
    nblk = n // NB
    rows = lax.broadcasted_iota(jnp.int32, (NB, NB), 0)
    lanes = lax.broadcasted_iota(jnp.int32, (NB, NB), 1)
    eye = jnp.where(rows == lanes, 1.0, 0.0)
    big[:, :n] = g_ref[...]
    big[:, n:] = jnp.zeros((n, n), jnp.float32)
    o_ref[...] = jnp.zeros((n, n), jnp.float32)

    def panel_step(p, carry):
        at = pl.multiple_of(p * NB, NB)
        wa[...] = big[pl.ds(at, NB), pl.ds(at, NB)]
        wx[...] = eye
        big[pl.ds(at, NB), pl.ds(pl.multiple_of(at + n, NB), NB)] = eye
        factor_block(wa, wx, linv)
        start = pl.multiple_of(at + NB, NB)
        y = jnp.dot(linv[...], big[pl.ds(at, NB), pl.ds(start, n)], precision=lax.Precision.HIGHEST, preferred_element_type=jnp.float32)
        big[pl.ds(at, NB), pl.ds(start, n)] = y

        def put(j, c):
            col = pl.multiple_of(j * NB, NB)
            o_ref[pl.ds(at, NB), pl.ds(col, NB)] = big[pl.ds(at, NB), pl.ds(pl.multiple_of(n + col, NB), NB)]
            return c
        lax.fori_loop(0, p + 1, put, 0)

        def trail(i, c):
            row = pl.multiple_of(i * NB, NB)
            left = big[pl.ds(at, NB), pl.ds(row, NB)]
            upd = lax.dot_general(left, big[pl.ds(at, NB), pl.ds(start, n)], (((0,), (0,)), ((), ())), precision=lax.Precision.HIGHEST, preferred_element_type=jnp.float32)
            big[pl.ds(row, NB), pl.ds(start, n)] = big[pl.ds(row, NB), pl.ds(start, n)] - upd
            return c
        lax.fori_loop(p + 1, nblk, trail, 0)
        return carry
    lax.fori_loop(0, nblk, panel_step, 0)


def chol_inverse(g):
    n = g.shape[0]
    return pl.pallas_call(
        chol_kernel,
        out_shape=jax.ShapeDtypeStruct((n, n), jnp.float32),
        in_specs=[pl.BlockSpec(memory_space=pltpu.VMEM)],
        out_specs=pl.BlockSpec(memory_space=pltpu.VMEM),
        scratch_shapes=[pltpu.VMEM((n, 2 * n), jnp.float32), pltpu.VMEM((NB, NB), jnp.float32),
                        pltpu.VMEM((NB, NB), jnp.float32), pltpu.VMEM((NB, NB), jnp.float32)],
        compiler_params=pltpu.CompilerParams(vmem_limit_bytes=40 * 2**20),
        name="chol_inverse",
    )(g)


AXES = ("tm", "slope")
RING = 4


def device_id(x, y, z, core):
    return ((x // 2) * 2 + core) * 32 + (x % 2) * 16 + z * 4 + y


def shift_pairs(dx=0, dy=0, dz=0, dc=0):
    return [
        (device_id(x, y, z, c), device_id((x + dx) % RING, (y + dy) % RING, (z + dz) % RING, (c + dc) % 2))
        for x in range(RING) for y in range(RING) for z in range(RING) for c in range(2)
    ]


def send(value, **shift):
    return lax.ppermute(value, AXES, shift_pairs(**shift))


def ring_gather(piece, axis_name, me, build):
    steps = [(1, send(piece, **{axis_name: 1})), (3, send(piece, **{axis_name: 3})), (2, send(piece, **{axis_name: 2}))]
    build(piece, me)
    for d, got in steps:
        build(got, (me + RING - d) % RING)


def gather_all(block, coords):
    x, y, z, core = coords
    rows, width = block.shape
    half = rows // 2
    by_x = jnp.zeros((2, 2, rows, width), block.dtype)

    def put_x(piece, at):
        nonlocal by_x
        by_x = lax.dynamic_update_slice(by_x, piece[None, None], (at // 2, at % 2, 0, 0))
    ring_gather(block, "dx", x, put_x)
    first, last = by_x[:, :, :half], by_x[:, :, half:]
    by_y = jnp.zeros((2, 2, RING, half, width), block.dtype)
    by_z = jnp.zeros((2, 2, RING, half, width), block.dtype)

    def put_y(piece, at):
        nonlocal by_y
        by_y = lax.dynamic_update_slice(by_y, piece[:, :, None], (0, 0, at, 0, 0))

    def put_z(piece, at):
        nonlocal by_z
        by_z = lax.dynamic_update_slice(by_z, piece[:, :, None], (0, 0, at, 0, 0))
    ring_gather(first, "dy", y, put_y)
    ring_gather(last, "dz", z, put_z)
    whole = jnp.zeros((2, 2, 2, RING, RING, 2, half, width), block.dtype)

    def put_first(piece, at):
        nonlocal whole
        for c, value in ((core, piece), (1 - core, send(piece, dc=1))):
            whole = lax.dynamic_update_slice(whole, value.reshape(2, 1, 2, 1, RING, 1, half, width), (0, c, 0, at, 0, 0, 0, 0))

    def put_last(piece, at):
        nonlocal whole
        for c, value in ((core, piece), (1 - core, send(piece, dc=1))):
            whole = lax.dynamic_update_slice(whole, value.reshape(2, 1, 2, RING, 1, 1, half, width), (0, c, 0, 0, at, 1, 0, 0))
    ring_gather(by_y, "dz", z, put_first)
    ring_gather(by_z, "dy", y, put_last)
    return whole.reshape(2, 2, 2, RING, RING, rows, width)


def shards(telemetry, frame_ids, valid, noise, prior_next):
    slope_index = lax.axis_index("slope")
    tm_index = lax.axis_index("tm")
    tel = telemetry[0]
    row_block, cycles, frames = tel.shape
    width = noise.shape[0]
    tm_count = 4
    quarter = row_block // tm_count
    frames_total = frames * tm_count
    coords = ((tm_index // 2) * 2 + slope_index // 16, slope_index % 4, (slope_index // 4) % 4, tm_index % 2)
    keep = lax.dynamic_slice(valid.reshape(cycles, 4), (0, slope_index // 8), (cycles, 1)).astype(jnp.bfloat16)
    onehot = (lax.broadcasted_iota(jnp.int32, (frames, frames), 0) == frame_ids[None, :]).astype(jnp.bfloat16)

    def select(rows, mask):
        return jnp.dot(rows, onehot, preferred_element_type=jnp.float32).astype(jnp.bfloat16) * mask
    first_own = select(tel[:, 0, :], keep[0])
    second_own = select(tel[:, 1, :], keep[1])
    first_cols = gather_all(first_own, coords).reshape(tm_count, width, frames)
    selected = select(tel.reshape(row_block * cycles, frames), jnp.tile(keep, (row_block, 1))).reshape(row_block, cycles, frames)
    second_rows = lax.all_to_all(second_own.reshape(tm_count, quarter, frames), "tm", 0, 0)
    selected, first_cols = lax.optimization_barrier((selected, first_cols))
    quarter_rows = lax.all_to_all(selected.reshape(tm_count, quarter, cycles, frames), "tm", 0, 0)

    def gram(rows):
        total = sum(lax.dot_general(rows[t], first_cols[t], (((rows.ndim - 2,), (1,)), ((), ())), preferred_element_type=jnp.float32) for t in range(tm_count))
        return total / float(frames_total)
    lead = gram(first_cols)
    ids = lax.broadcasted_iota(jnp.int32, (width, width), 0)
    lead = lead + jnp.where(ids == lax.broadcasted_iota(jnp.int32, (width, width), 1), noise[None, :], 0.0)
    second_gram = gram(second_rows)
    second_all = gather_all(second_gram, coords)
    second_all = second_all.transpose(2, 3, 4, 0, 1, 5, 6).reshape(width, width)
    inverse = chol_inverse(lead)
    block = gram(quarter_rows)
    diag_ids = slope_index * row_block + tm_index * quarter + lax.broadcasted_iota(jnp.int32, (quarter, width), 0)
    diag = jnp.where(diag_ids == lax.broadcasted_iota(jnp.int32, (quarter, width), 1), noise[None, :], 0.0)
    block = block.at[:, 0, :].add(diag)
    high = lax.Precision.HIGH
    second = lax.dot_general(second_all, inverse, (((1,), (1,)), ((), ())), precision=high)
    panel = lax.dot_general(block, inverse, (((2,), (1,)), ((), ())), precision=high)
    update = lax.dot_general(panel, second, (((2,), (1,)), ((), ())), precision=high)
    return panel[None], (prior_next[0] - update)[None]


def solution(mesh):
    return jax.shard_map(
        shards,
        mesh=mesh,
        in_specs=(P("slope", None, None, "tm"), P("tm"), P(), P(), P("slope", "tm", None, None)),
        out_specs=(P("slope", "tm", None, None), P("slope", "tm", None, None)),
        check_vma=False,
    )
```

```python
import jax
import jax.numpy as jnp
from jax import lax
from jax.experimental import pallas as pl
from jax.experimental.pallas import tpu as pltpu
from jax.sharding import PartitionSpec as P

NB = 128
MB = 8
TN = (((0,), (0,)), ((), ()))
NT = (((1,), (1,)), ((), ()))
WHOLE = pl.BlockSpec(memory_space=pltpu.VMEM)


def params(mib=40):
    return pltpu.CompilerParams(vmem_limit_bytes=mib * 2**20)


def bf16_round(z):
    return z.astype(jnp.bfloat16).astype(jnp.float32)


def split3(z):
    high = bf16_round(z)
    rest = z - high
    mid = bf16_round(rest)
    return high, mid, rest - mid


def row_of(z, j):
    return jnp.broadcast_to(z[j:j + 1, :], z.shape)


def factor_block(wa, wx, out):
    sub = lax.broadcasted_iota(jnp.int32, (MB, NB), 0)
    a = wa[0:MB, :]
    x = wx[0:MB, :]
    for k in range(NB // MB):
        lo = MB * k
        after = lo + MB < NB
        cols = [jnp.broadcast_to(a[:, lo + j:lo + j + 1], (MB, NB)) for j in range(MB)]
        if after:
            na = wa[lo + MB:lo + 2 * MB, :]
            nx = wx[lo + MB:lo + 2 * MB, :]
            ncols = [jnp.broadcast_to(na[:, lo + j:lo + j + 1], (MB, NB)) for j in range(MB)]
        inv_d = jnp.zeros((MB, NB), jnp.float32)
        piv = jnp.zeros((MB, NB), jnp.float32)
        for j in range(MB):
            pivot = row_of(cols[j], j)
            recip = 1.0 / pivot
            mult = jnp.where(sub > j, cols[j] * recip, 0.0)
            ra, rx = row_of(a, j), row_of(x, j)
            if after:
                nmult = ncols[j] * recip
                na = na - nmult * ra
                nx = nx - nmult * rx
            for l in range(j + 1, MB):
                rc = row_of(cols[l], j)
                cols[l] = cols[l] - mult * rc
                if after:
                    ncols[l] = ncols[l] - nmult * rc
            a = a - mult * ra
            x = x - mult * rx
            inv_d = jnp.where(sub == j, recip, inv_d)
            piv = jnp.where(sub == j, pivot, piv)
        out[lo:lo + MB, :] = x * (1.0 / jnp.sqrt(piv))
        if lo + 2 * MB < NB:
            top = lo + 2 * MB
            right = jnp.concatenate([a * inv_d, x * inv_d], axis=1)
            lh, lm, ll = split3(a)
            rh, rm, rl = split3(right)
            left_stack = jnp.concatenate([lh, lh, lm, lh, ll, lm], axis=0).astype(jnp.bfloat16)
            right_stack = jnp.concatenate([rh, rm, rh, rl, rh, rm], axis=0).astype(jnp.bfloat16)
            prod = lax.dot_general(left_stack, right_stack, TN, preferred_element_type=jnp.float32)
            wa[top:, :] = wa[top:, :] - prod[top:, :NB]
            wx[top:, :] = wx[top:, :] - prod[top:, NB:]
        if after:
            a, x = na, nx


def chol_panels(first, count, big, wa, wx, linv, ys):
    n = big.shape[0]
    nblk = n // NB
    rows = lax.broadcasted_iota(jnp.int32, (NB, NB), 0)
    lanes = lax.broadcasted_iota(jnp.int32, (NB, NB), 1)
    eye = jnp.where(rows == lanes, 1.0, 0.0)

    def panel_step(p, carry):
        at = pl.multiple_of(p * NB, NB)
        wa[...] = big[pl.ds(at, NB), pl.ds(at, NB)]
        wx[...] = eye
        big[pl.ds(at, NB), pl.ds(at, NB)] = eye
        factor_block(wa, wx, linv)
        y = jnp.dot(linv[...], big[pl.ds(at, NB), :], precision=lax.Precision.HIGHEST, preferred_element_type=jnp.float32)
        big[pl.ds(at, NB), :] = y
        high, mid, low = (part.astype(jnp.bfloat16) for part in split3(y))
        for i, part in enumerate((high, mid, low, high)):
            ys[i * NB:(i + 1) * NB, :] = part

        def trail(i, c):
            row = pl.multiple_of(i * NB, NB)
            big[pl.ds(row, NB), pl.ds(at, NB)] = jnp.zeros((NB, NB), jnp.float32)
            hm = ys[0:2 * NB, pl.ds(row, NB)]
            mh = jnp.concatenate([ys[NB:2 * NB, pl.ds(row, NB)], ys[0:NB, pl.ds(row, NB)]], axis=0)
            lh = ys[2 * NB:4 * NB, pl.ds(row, NB)]
            hl = jnp.concatenate([ys[0:NB, :], ys[2 * NB:3 * NB, :]], axis=0)
            dot = lambda u, v: lax.dot_general(u, v, TN, preferred_element_type=jnp.float32)
            upd = dot(hm, ys[0:2 * NB, :]) + (dot(mh, ys[0:2 * NB, :]) + dot(lh, hl))
            big[pl.ds(row, NB), :] = big[pl.ds(row, NB), :] - upd
            return c

        lax.fori_loop(p + 1, nblk, trail, 0)
        return carry

    lax.fori_loop(first, first + count, panel_step, 0)


CHOL_SCRATCH = [pltpu.VMEM((NB, NB), jnp.float32)] * 3


def chol_step(big, first, count):
    n = big.shape[0]

    def kernel(src, dst, wa, wx, linv, ys):
        chol_panels(first, count, dst, wa, wx, linv, ys)

    return pl.pallas_call(
        kernel, out_shape=jax.ShapeDtypeStruct(big.shape, jnp.float32), in_specs=[WHOLE], out_specs=WHOLE,
        scratch_shapes=CHOL_SCRATCH + [pltpu.VMEM((4 * NB, n), jnp.bfloat16)], input_output_aliases={0: 0},
        compiler_params=params(), name="chol_panels")(big)


SPLIT = (2, 5, 1)
AXES = ("tm", "slope")
RING = 4
SCALARS = pl.BlockSpec(memory_space=pltpu.SMEM)


def pick_first(tel, ids, keep, core):
    rows, _, frames = tel.shape
    half = rows // 2

    def kernel(core_ref, tel_ref, ids_ref, keep_ref, mine_ref, theirs_ref, second_ref, hot_ref, got, lead):
        hot_ref[...] = jnp.where(lax.broadcasted_iota(jnp.int32, (frames, frames), 0) == ids_ref[...], 1.0, 0.0).astype(jnp.bfloat16)
        got[...] = jnp.dot(tel_ref[...].reshape(rows * 16, frames), hot_ref[...], preferred_element_type=jnp.float32).reshape(rows, 16, frames)
        lead[...] = got[:, 0, :] * keep_ref[0:1, 0:1]
        at = pl.multiple_of(core_ref[0] * half, half)
        mine_ref[...] = lead[pl.ds(at, half), :].astype(jnp.bfloat16)
        theirs_ref[...] = lead[pl.ds(pl.multiple_of(half - at, half), half), :].astype(jnp.bfloat16)
        second_ref[...] = (got[:, 1, :] * keep_ref[1:2, 0:1]).astype(jnp.bfloat16)

    whole = lambda shape: pl.BlockSpec(shape, lambda i: (0,) * len(shape))
    shapes = ((half, frames), (half, frames), (rows, frames), (frames, frames))
    return pl.pallas_call(
        kernel,
        grid=(1,),
        out_shape=tuple(jax.ShapeDtypeStruct(s, jnp.bfloat16) for s in shapes),
        in_specs=[SCALARS, pl.BlockSpec((rows, 16, frames), lambda i: (0, 0, 0)), whole((1, frames)), whole(keep.shape)],
        out_specs=tuple(whole(s) for s in shapes),
        scratch_shapes=[pltpu.VMEM((rows, 16, frames), jnp.float32), pltpu.VMEM((rows, frames), jnp.float32)],
        compiler_params=params(), name="pick_first")(core, tel, ids, keep)


def pick_all(tel, hot, keep, tm_index):
    rows, cycles, frames = tel.shape
    per = 4
    quarter = rows // RING
    steps = quarter // per

    def kernel(tm_ref, tel_ref, hot_ref, keep_ref, *outs):
        got = jnp.dot(tel_ref[...].reshape(per * cycles, frames), hot_ref[...], preferred_element_type=jnp.float32)
        got = (got.reshape(per, cycles, frames) * keep_ref[...][None]).astype(jnp.bfloat16)
        for k in range(RING):
            @pl.when(pl.program_id(0) // steps == k)
            def _():
                outs[k][...] = got

    place = lambda k: pl.BlockSpec((per, cycles, frames), lambda i, tm: (jnp.clip(i - steps * k, 0, steps - 1), 0, 0))
    return pl.pallas_call(
        kernel, out_shape=(jax.ShapeDtypeStruct((quarter, cycles, frames), jnp.bfloat16),) * RING,
        grid_spec=pltpu.PrefetchScalarGridSpec(
            num_scalar_prefetch=1, grid=(rows // per,),
            in_specs=[pl.BlockSpec((per, cycles, frames), lambda i, tm: (jnp.bitwise_xor(tm[0], i // steps) * steps + i % steps, 0, 0)),
                      pl.BlockSpec((frames, frames), lambda i, tm: (0, 0)), pl.BlockSpec(keep.shape, lambda i, tm: (0, 0))],
            out_specs=tuple(place(k) for k in range(RING))),
        compiler_params=params(), name="pick_all")(tm_index, tel, hot, keep)


def lead_gram(own, other, second_rows, noise, place):
    width = noise.shape[1]
    tm_count, quarter, frames = second_rows.shape
    half = own[0].shape[3]
    scale = 1.0 / (tm_count * frames)
    group = 2 * RING

    def kernel(place_ref, *refs):
        parts = (refs[:RING], refs[RING:2 * RING])
        rows_ref, noise_ref, cols_hbm, gram_ref, second_ref, left, acc, arrive, leave = refs[2 * RING:]
        me_core, me_x, me_y, me_z = (place_ref[i] for i in range(4))

        def fetch(t, slot):
            x_hi, c = t // 2, t % 2
            for kind in range(2):
                by = me_core if kind == 0 else 1 - me_core
                on_z = by == 0
                outer_me, inner_me = jnp.where(on_z, me_z, me_y), jnp.where(on_z, me_y, me_z)
                outer_step, inner_step = jnp.where(on_z, width // 8, width // 32), jnp.where(on_z, width // 32, width // 8)
                shift_c = (by + c) % 2
                for x_lo in range(2):
                    shift_x = (me_x + RING - x_hi * 2 - x_lo) % RING
                    for i in range(RING):
                        for q in range(RING):
                            at = x_lo * (width // 2) + ((outer_me + RING - i) % RING) * outer_step + ((inner_me + RING - q) % RING) * inner_step + by * half
                            pltpu.make_async_copy(parts[kind][i].at[q, shift_x, shift_c], left.at[slot, pl.ds(pl.multiple_of(at, half), half)], arrive.at[slot]).start()

        def out_copy(t, slot):
            return pltpu.make_async_copy(left.at[slot, pl.ds(0, width)], cols_hbm.at[t], leave.at[slot])

        for slot in range(2):
            left[slot, width:, :] = jnp.zeros((16, frames), jnp.bfloat16)
        fetch(0, 0)

        def one(t, carry):
            slot = t % 2

            @pl.when(jnp.logical_and(t >= 1, t + 1 < tm_count))
            def _():
                out_copy(t - 1, 1 - slot).wait()

            @pl.when(t + 1 < tm_count)
            def _():
                fetch(t + 1, 1 - slot)

            pltpu.make_async_copy(cols_hbm.at[0], left.at[slot, pl.ds(0, width)], arrive.at[slot]).wait()
            left[slot, width:width + quarter, :] = rows_ref[t]
            out_copy(t, slot).start()
            part = lax.dot_general(left[slot], left[slot, :width, :], NT, preferred_element_type=jnp.float32)

            @pl.when(t == 0)
            def _():
                acc[...] = part

            @pl.when(t > 0)
            def _():
                acc[...] += part

            return carry

        lax.fori_loop(0, tm_count, one, 0)
        rows = lax.broadcasted_iota(jnp.int32, (width, width), 0)
        diag = rows == lax.broadcasted_iota(jnp.int32, (width, width), 1)
        gram_ref[...] = acc[:width, :] * scale + jnp.where(diag, noise_ref[...], 0.0)
        second = acc[width:width + quarter, :] * scale
        for i in range(group):
            second_ref[i] = second
        out_copy(tm_count - 2, 0).wait()
        out_copy(tm_count - 1, 1).wait()

    anywhere = pl.BlockSpec(memory_space=pl.ANY)
    return pl.pallas_call(
        kernel,
        out_shape=(jax.ShapeDtypeStruct((tm_count, width, frames), jnp.bfloat16), jax.ShapeDtypeStruct((width, width), jnp.float32),
                   jax.ShapeDtypeStruct((group, quarter, width), jnp.float32)),
        in_specs=[SCALARS] + [anywhere] * (2 * RING) + [WHOLE] * 2,
        out_specs=(anywhere, WHOLE, WHOLE),
        scratch_shapes=[pltpu.VMEM((2, width + 16, frames), jnp.bfloat16), pltpu.VMEM((width + 16, width), jnp.float32),
                        pltpu.SemaphoreType.DMA((2,)), pltpu.SemaphoreType.DMA((2,))],
        compiler_params=params(40), name="lead_gram")(place, *own, *other, second_rows, noise)


def two(z):
    high = z.astype(jnp.bfloat16)
    return high, (z - high.astype(jnp.float32)).astype(jnp.bfloat16)


def dot3(left, right):
    dot = lambda p, q: lax.dot_general(p, q, NT, preferred_element_type=jnp.float32)
    return dot(left[0], right[0]) + (dot(left[0], right[1]) + dot(left[1], right[0]))


STRIPS = 4


def lower_dot3(left_refs, right_refs, put):
    n = right_refs[0].shape[0]
    step = n // STRIPS
    for s in range(STRIPS):
        rows, k = pl.ds(s * step, step), (s + 1) * step
        put(s * step, step, dot3([r[:, :k] for r in left_refs], [r[rows, :k] for r in right_refs]))


def second_block(mine, theirs, big, core):
    width = big.shape[0]
    half = width // 2
    plane, group = mine.shape[:2]

    def kernel(core_ref, mine_ref, theirs_ref, inv_ref, sh_ref, sl_ref, ih_ref, il_ref, g, gl):
        ih_ref[...], il_ref[...] = two(jnp.where(lax.broadcasted_iota(jnp.int32, (width, width), 0) >= lax.broadcasted_iota(jnp.int32, (width, width), 1), inv_ref[...], 0.0))
        left = core_ref[0] == 0
        for zy in range(plane):
            for xc in range(group):
                at = (xc // 2 % 2) * half + zy * (width // 32) + (xc // 4) * 16 + (xc % 2) * 8
                u, v = mine_ref[zy, xc], theirs_ref[zy, xc]
                g[at:at + 8, :half] = jnp.where(left, u, v)
                g[at:at + 8, half:] = jnp.where(left, v, u)
        gl[0], gl[1] = two(g[...])

        def put(at, size, value):
            sh_ref[:, at:at + size], sl_ref[:, at:at + size] = two(value)

        lower_dot3([gl.at[0], gl.at[1]], [ih_ref, il_ref], put)

    out = jax.ShapeDtypeStruct((width, width), jnp.bfloat16)
    return pl.pallas_call(
        kernel,
        out_shape=(out,) * 4,
        in_specs=[SCALARS] + [WHOLE] * 3,
        out_specs=(WHOLE,) * 4,
        scratch_shapes=[pltpu.VMEM((width, width), jnp.float32), pltpu.VMEM((2, width, width), jnp.bfloat16)],
        compiler_params=params(50), name="second_block")(core, mine, theirs, big)


def finish(rows, cols, diag, second, inverse, prior, tm_index):
    quarter, cycles, frames = rows[0].shape
    width = cols.shape[1]
    count = quarter * cycles
    scale = 1.0 / (RING * frames)

    def kernel(tm_ref, r0, r1, r2, r3, cols_ref, diag_ref, sh_ref, sl_ref, ih_ref, il_ref, prior_hbm, panel_hbm, next_hbm, rows_v, acc, gh, gl, prior_v, sems, row_sems):
        k = pl.program_id(0)
        fetch = pltpu.make_async_copy(prior_hbm, prior_v, sems.at[0])

        @pl.when(k == 0)
        def _():
            for i, r in enumerate((r0, r1, r2, r3)):
                pltpu.make_async_copy(r, rows_v.at[i], row_sems.at[i]).start()
            fetch.start()

        pltpu.make_async_copy(r0, rows_v.at[k], row_sems.at[k]).wait()
        part = lax.dot_general(rows_v[k].reshape(count, frames), cols_ref[0], NT, preferred_element_type=jnp.float32)

        @pl.when(k == 0)
        def _():
            acc[...] = part.reshape(acc.shape)

        @pl.when(k > 0)
        def _():
            acc[...] += part.reshape(acc.shape)

        @pl.when(k == RING - 1)
        def _():
            cycle = lax.broadcasted_iota(jnp.int32, (1, cycles, width), 1)
            gram = acc[...] * scale + jnp.where(cycle == 0, diag_ref[...], 0.0)
            gh[...], gl[...] = two(gram.reshape(count, width))

            def put(at, size, value):
                acc[:, :, at:at + size] = value.reshape(quarter, cycles, size)

            lower_dot3([gh, gl], [ih_ref, il_ref], put)
            send_panel = pltpu.make_async_copy(acc, panel_hbm, sems.at[1])
            send_panel.start()
            gh[...], gl[...] = two(acc[...].reshape(count, width))
            fetch.wait()
            step = width // STRIPS
            for s in range(STRIPS):
                cut = pl.ds(s * step, step)
                update = dot3([gh[...], gl[...]], [sh_ref[cut, :], sl_ref[cut, :]])
                prior_v[:, :, s * step:(s + 1) * step] = prior_v[:, :, s * step:(s + 1) * step] - update.reshape(quarter, cycles, step)
            send_next = pltpu.make_async_copy(prior_v, next_hbm, sems.at[2])
            send_next.start()
            send_panel.wait()
            send_next.wait()

    whole2 = pl.BlockSpec((width, width), lambda i, tm: (0, 0), pipeline_mode=pl.Buffered(1))
    anywhere = pl.BlockSpec(memory_space=pl.ANY)
    out = jax.ShapeDtypeStruct((quarter, cycles, width), jnp.float32)
    return pl.pallas_call(
        kernel,
        out_shape=(out, out),
        grid_spec=pltpu.PrefetchScalarGridSpec(
            num_scalar_prefetch=1, grid=(RING,),
            in_specs=[anywhere] * RING + [pl.BlockSpec((1, width, frames), lambda i, tm: (jnp.bitwise_xor(tm[0], i), 0, 0)),
                      pl.BlockSpec((quarter, 1, width), lambda i, tm: (0, 0, 0))] + [whole2] * 4 + [anywhere],
            out_specs=(anywhere, anywhere),
            scratch_shapes=[pltpu.VMEM((RING, quarter, cycles, frames), jnp.bfloat16), pltpu.VMEM((quarter, cycles, width), jnp.float32)]
            + [pltpu.VMEM((count, width), jnp.bfloat16)] * 2
            + [pltpu.VMEM((quarter, cycles, width), jnp.float32), pltpu.SemaphoreType.DMA((3,)), pltpu.SemaphoreType.DMA((RING,))]),
        compiler_params=params(50), name="finish")(tm_index, *rows, cols, diag, *second, *inverse, prior)


def device_id(x, y, z, core):
    return ((x // 2) * 2 + core) * 32 + (x % 2) * 16 + z * 4 + y


DEVICES = [(x, y, z, c) for x in range(RING) for y in range(RING) for z in range(RING) for c in range(2)]


def send(value, step):
    return lax.ppermute(value, AXES, [(device_id(*d), device_id(*step(*d))) for d in DEVICES])


def swap_cores(value):
    return send(value, lambda x, y, z, c: (x, y, z, 1 - c))


def around(value, step):
    return [value] + [send(value, step(d)) for d in range(1, RING)]


def x_ring(d):
    return lambda x, y, z, c: ((x + d) % RING, y, z, c)


def inner_ring(d):
    return lambda x, y, z, c: (x, (y + d * (1 - c)) % RING, (z + d * c) % RING, c)


def outer_ring(d):
    return lambda x, y, z, c: (x, (y + d * c) % RING, (z + d * (1 - c)) % RING, c)


def flip_tm(k):
    return lambda x, y, z, c: (x ^ (k & 2), y, z, c ^ (k & 1))


CHIP_ROWS = [[device_id(x, y, z, c) for x in range(RING) for c in range(2)] for z in range(RING) for y in range(RING)]
PLANES = [[device_id(x, y, z, c) for z in range(RING) for y in range(RING)] for x in range(RING) for c in range(2)]


def shards(telemetry, frame_ids, valid, noise, prior_next):
    slope_index = lax.axis_index("slope")
    tm_index = lax.axis_index("tm")
    tel = telemetry[0]
    row_block, cycles, frames = tel.shape
    width = noise.shape[0]
    tm_count = 4
    quarter = row_block // tm_count
    core_index = tm_index % 2
    core = core_index.reshape(1)
    place = jnp.stack([core_index, (tm_index // 2) * 2 + slope_index // 16, slope_index % 4, (slope_index // 4) % 4])
    keep = lax.dynamic_slice(valid.reshape(cycles, 4), (0, slope_index // 8), (cycles, 1)).astype(jnp.float32)
    mine, theirs, second_own, hot = pick_first(tel, frame_ids[None, :], keep, core)
    pair = jnp.stack([mine, swap_cores(theirs)])
    by_x = jnp.stack(around(pair, x_ring))
    by_inner = jnp.stack(around(by_x, inner_ring))
    by_inner, hot, second_own = lax.optimization_barrier((by_inner, hot, second_own))
    own = around(by_inner, outer_ring)
    second_rows = lax.all_to_all(second_own.reshape(tm_count, quarter, frames), "tm", 0, 0)
    selected = pick_all(tel, hot, keep, tm_index.reshape(1))
    other = [swap_cores(piece) for piece in own]
    selected, own, other = lax.optimization_barrier((selected, own, other))
    rows = [selected[0], None, send(selected[2], flip_tm(2)), None]
    first_cols, lead, second_gram = lead_gram(own, other, second_rows, noise[None, :], place)
    near = lax.all_to_all(second_gram, AXES, 0, 0, axis_index_groups=CHIP_ROWS)
    big = chol_step(lead, 0, SPLIT[0])
    near, big, selected = lax.optimization_barrier((near, big, selected))
    rows[3] = send(selected[3], flip_tm(3))
    rows[1] = send(selected[1], flip_tm(1))
    near = lax.dynamic_slice_in_dim(near, core_index * (width // 2), width // 2, axis=2)
    near = jnp.broadcast_to(near[None], (16,) + near.shape)
    mine2 = lax.all_to_all(near, AXES, 0, 0, axis_index_groups=PLANES)
    big = chol_step(big, SPLIT[0], SPLIT[1])
    mine2, big = lax.optimization_barrier((mine2, big))
    theirs2 = swap_cores(mine2)
    big = chol_step(big, SPLIT[0] + SPLIT[1], SPLIT[2])
    split = second_block(mine2, theirs2, big, core)
    diag_ids = slope_index * row_block + tm_index * quarter + lax.broadcasted_iota(jnp.int32, (quarter, 1, width), 0)
    diag = jnp.where(diag_ids == lax.broadcasted_iota(jnp.int32, (quarter, 1, width), 2), noise[None, None, :], 0.0)
    panel, next_block = finish(rows, first_cols, diag, split[:2], split[2:], prior_next[0], tm_index.reshape(1))
    return panel[None], next_block[None]


def solution(mesh):
    return jax.shard_map(
        shards,
        mesh=mesh,
        in_specs=(P("slope", None, None, "tm"), P("tm"), P(), P(), P("slope", "tm", None, None)),
        out_specs=(P("slope", "tm", None, None), P("slope", "tm", None, None)),
        check_vma=False,
    )
```

```python
import jax
import jax.numpy as jnp
from jax import lax
from jax.experimental import pallas as pl
from jax.experimental.pallas import tpu as pltpu
from jax.sharding import PartitionSpec as P

NB = 128
MB = 8
TN = (((0,), (0,)), ((), ()))
NT = (((1,), (1,)), ((), ()))
WHOLE = pl.BlockSpec(memory_space=pltpu.VMEM)


def in_hbm(value):
    return pltpu.with_memory_space_constraint(value, pltpu.HBM)


def params(mib=40):
    return pltpu.CompilerParams(vmem_limit_bytes=mib * 2**20)


def bf16_round(z):
    return z.astype(jnp.bfloat16).astype(jnp.float32)


def split3(z):
    high = bf16_round(z)
    rest = z - high
    mid = bf16_round(rest)
    return high, mid, rest - mid


def row_of(z, j):
    return jnp.broadcast_to(z[j:j + 1, :], z.shape)


def factor_block(wa, wx, out):
    sub = lax.broadcasted_iota(jnp.int32, (MB, NB), 0)
    a = wa[0:MB, :]
    x = wx[0:MB, :]
    for k in range(NB // MB):
        lo = MB * k
        after = lo + MB < NB
        cols = [jnp.broadcast_to(a[:, lo + j:lo + j + 1], (MB, NB)) for j in range(MB)]
        if after:
            na = wa[lo + MB:lo + 2 * MB, :]
            nx = wx[lo + MB:lo + 2 * MB, :]
            ncols = [jnp.broadcast_to(na[:, lo + j:lo + j + 1], (MB, NB)) for j in range(MB)]
        inv_d = jnp.zeros((MB, NB), jnp.float32)
        piv = jnp.zeros((MB, NB), jnp.float32)
        for j in range(MB):
            pivot = row_of(cols[j], j)
            recip = 1.0 / pivot
            mult = jnp.where(sub > j, cols[j] * recip, 0.0)
            ra, rx = row_of(a, j), row_of(x, j)
            if after:
                nmult = ncols[j] * recip
                na = na - nmult * ra
                nx = nx - nmult * rx
            for l in range(j + 1, MB):
                rc = row_of(cols[l], j)
                cols[l] = cols[l] - mult * rc
                if after:
                    ncols[l] = ncols[l] - nmult * rc
            a = a - mult * ra
            x = x - mult * rx
            inv_d = jnp.where(sub == j, recip, inv_d)
            piv = jnp.where(sub == j, pivot, piv)
        out[lo:lo + MB, :] = x * (1.0 / jnp.sqrt(piv))
        if lo + 2 * MB < NB:
            top = lo + 2 * MB
            right = jnp.concatenate([a * inv_d, x * inv_d], axis=1)
            lh, lm, ll = split3(a)
            rh, rm, rl = split3(right)
            left_stack = jnp.concatenate([lh, lh, lm, lh, ll, lm], axis=0).astype(jnp.bfloat16)
            right_stack = jnp.concatenate([rh, rm, rh, rl, rh, rm], axis=0).astype(jnp.bfloat16)
            prod = lax.dot_general(left_stack, right_stack, TN, preferred_element_type=jnp.float32)
            wa[top:, :] = wa[top:, :] - prod[top:, :NB]
            wx[top:, :] = wx[top:, :] - prod[top:, NB:]
        if after:
            a, x = na, nx


def chol_panels(first, count, src, dst, big, wa, wx, linv, ys, arrive, leave):
    n = big.shape[0]
    nblk = n // NB
    last = first + count - 1
    rows = lax.broadcasted_iota(jnp.int32, (NB, NB), 0)
    lanes = lax.broadcasted_iota(jnp.int32, (NB, NB), 1)
    eye = jnp.where(rows == lanes, 1.0, 0.0)

    def block(i):
        return pl.ds(pl.multiple_of(i * NB, NB), NB)

    def load(i):
        return pltpu.make_async_copy(src.at[block(i)], big.at[block(i)], arrive.at[i])

    def store(i):
        return pltpu.make_async_copy(big.at[block(i)], dst.at[block(i)], leave.at[i])

    for i in range(first, nblk):
        load(i).start()
    load(first).wait()

    def panel_step(p, carry):
        at = pl.multiple_of(p * NB, NB)
        wa[...] = big[pl.ds(at, NB), pl.ds(at, NB)]
        wx[...] = eye
        big[pl.ds(at, NB), pl.ds(at, NB)] = eye
        factor_block(wa, wx, linv)
        y = jnp.dot(linv[...], big[pl.ds(at, NB), :], precision=lax.Precision.HIGHEST, preferred_element_type=jnp.float32)
        big[pl.ds(at, NB), :] = y
        store(p).start()
        high, mid, low = (part.astype(jnp.bfloat16) for part in split3(y))
        for i, part in enumerate((high, mid, low, high)):
            ys[i * NB:(i + 1) * NB, :] = part

        def trail(i, c):
            row = pl.multiple_of(i * NB, NB)

            @pl.when(p == first)
            def _():
                load(i).wait()

            big[pl.ds(row, NB), pl.ds(at, NB)] = jnp.zeros((NB, NB), jnp.float32)
            hm = ys[0:2 * NB, pl.ds(row, NB)]
            mh = jnp.concatenate([ys[NB:2 * NB, pl.ds(row, NB)], ys[0:NB, pl.ds(row, NB)]], axis=0)
            lh = ys[2 * NB:4 * NB, pl.ds(row, NB)]
            hl = jnp.concatenate([ys[0:NB, :], ys[2 * NB:3 * NB, :]], axis=0)
            dot = lambda u, v: lax.dot_general(u, v, TN, preferred_element_type=jnp.float32)
            upd = dot(hm, ys[0:2 * NB, :]) + (dot(mh, ys[0:2 * NB, :]) + dot(lh, hl))
            big[pl.ds(row, NB), :] = big[pl.ds(row, NB), :] - upd

            @pl.when(p == last)
            def _():
                store(i).start()

            return c

        lax.fori_loop(p + 1, nblk, trail, 0)
        return carry

    lax.fori_loop(first, last + 1, panel_step, 0)
    for i in range(first, nblk):
        store(i).wait()


CHOL_SCRATCH = [pltpu.VMEM((NB, NB), jnp.float32)] * 3


def chol_step(src, first, count):
    n = src.shape[0]
    blocks = n // NB

    def kernel(src_ref, dst_ref, big, wa, wx, linv, ys, arrive, leave):
        chol_panels(first, count, src_ref, dst_ref, big, wa, wx, linv, ys, arrive, leave)

    hbm = pl.BlockSpec(memory_space=pltpu.HBM)
    return pl.pallas_call(
        kernel, out_shape=pltpu.HBM((n, n), jnp.float32), in_specs=[hbm], out_specs=hbm,
        scratch_shapes=[pltpu.VMEM((n, n), jnp.float32)] + CHOL_SCRATCH
        + [pltpu.VMEM((4 * NB, n), jnp.bfloat16), pltpu.SemaphoreType.DMA((blocks,)), pltpu.SemaphoreType.DMA((blocks,))],
        input_output_aliases={0: 0}, compiler_params=params(24), name="chol_panels")(in_hbm(src))


SPLIT = (2, 5, 1)
AXES = ("tm", "slope")
RING = 4
SCALARS = pl.BlockSpec(memory_space=pltpu.SMEM)
HBM = pl.BlockSpec(memory_space=pltpu.HBM)


def pick_first(tel, ids, keep, core):
    rows, _, frames = tel.shape
    half = rows // 2

    def kernel(core_ref, tel_hbm, ids_ref, keep_ref, mine_ref, theirs_ref, second_ref, hot_ref, got, lead, tel_ref, sem):
        fetch = pltpu.make_async_copy(tel_hbm.at[:, pl.ds(0, 16), :], tel_ref, sem)
        fetch.start()
        hot_ref[...] = jnp.where(lax.broadcasted_iota(jnp.int32, (frames, frames), 0) == ids_ref[...], 1.0, 0.0).astype(jnp.bfloat16)
        fetch.wait()
        got[...] = jnp.dot(tel_ref[...].reshape(rows * 16, frames), hot_ref[...], preferred_element_type=jnp.float32).reshape(rows, 16, frames)
        lead[...] = got[:, 0, :] * keep_ref[0:1, 0:1]
        at = pl.multiple_of(core_ref[0] * half, half)
        mine_ref[...] = lead[pl.ds(at, half), :].astype(jnp.bfloat16)
        theirs_ref[...] = lead[pl.ds(pl.multiple_of(half - at, half), half), :].astype(jnp.bfloat16)
        second_ref[...] = (got[:, 1, :] * keep_ref[1:2, 0:1]).astype(jnp.bfloat16)

    whole = lambda shape: pl.BlockSpec(shape, lambda i: (0,) * len(shape))
    shapes = ((half, frames), (half, frames), (rows, frames), (frames, frames))
    return pl.pallas_call(
        kernel,
        grid=(1,),
        out_shape=tuple(jax.ShapeDtypeStruct(s, jnp.bfloat16) for s in shapes),
        in_specs=[SCALARS, HBM, whole((1, frames)), whole(keep.shape)],
        out_specs=tuple(whole(s) for s in shapes),
        scratch_shapes=[pltpu.VMEM((rows, 16, frames), jnp.float32), pltpu.VMEM((rows, frames), jnp.float32),
                        pltpu.VMEM((rows, 16, frames), tel.dtype), pltpu.SemaphoreType.DMA],
        compiler_params=params(), name="pick_first")(core, in_hbm(tel), ids, keep)


def pick_all(tel, hot, keep, tm_index):
    rows, cycles, frames = tel.shape
    per = 4
    quarter = rows // RING
    steps = quarter // per

    def kernel(tm_ref, tel_ref, hot_ref, keep_ref, *outs):
        got = jnp.dot(tel_ref[...].reshape(per * cycles, frames), hot_ref[...], preferred_element_type=jnp.float32)
        got = (got.reshape(per, cycles, frames) * keep_ref[...][None]).astype(jnp.bfloat16)
        for k in range(RING):
            @pl.when(pl.program_id(0) // steps == k)
            def _():
                outs[k][...] = got

    place = lambda k: pl.BlockSpec((per, cycles, frames), lambda i, tm: (jnp.clip(i - steps * k, 0, steps - 1), 0, 0))
    return pl.pallas_call(
        kernel, out_shape=(pltpu.HBM((quarter, cycles, frames), jnp.bfloat16),) * RING,
        grid_spec=pltpu.PrefetchScalarGridSpec(
            num_scalar_prefetch=1, grid=(rows // per,),
            in_specs=[pl.BlockSpec((per, cycles, frames), lambda i, tm: (jnp.bitwise_xor(tm[0], i // steps) * steps + i % steps, 0, 0)),
                      pl.BlockSpec((frames, frames), lambda i, tm: (0, 0)), pl.BlockSpec(keep.shape, lambda i, tm: (0, 0))],
            out_specs=tuple(place(k) for k in range(RING))),
        compiler_params=params(), name="pick_all")(tm_index, in_hbm(tel), hot, keep)


def lead_gram(own, other, second_rows, noise, place):
    width = noise.shape[1]
    tm_count, quarter, frames = second_rows.shape
    half = own[0].shape[3]
    scale = 1.0 / (tm_count * frames)
    group = 2 * RING

    def kernel(place_ref, *refs):
        parts = (refs[:RING], refs[RING:2 * RING])
        rows_ref, noise_ref, cols_hbm, gram_hbm, second_ref, left, acc, arrive, leave, gram_sem = refs[2 * RING:]
        me_core, me_x, me_y, me_z = (place_ref[i] for i in range(4))

        def fetch(t, slot):
            x_hi, c = t // 2, t % 2
            for kind in range(2):
                by = me_core if kind == 0 else 1 - me_core
                on_z = by == 0
                outer_me, inner_me = jnp.where(on_z, me_z, me_y), jnp.where(on_z, me_y, me_z)
                outer_step, inner_step = jnp.where(on_z, width // 8, width // 32), jnp.where(on_z, width // 32, width // 8)
                shift_c = (by + c) % 2
                for x_lo in range(2):
                    shift_x = (me_x + RING - x_hi * 2 - x_lo) % RING
                    for i in range(RING):
                        for q in range(RING):
                            at = x_lo * (width // 2) + ((outer_me + RING - i) % RING) * outer_step + ((inner_me + RING - q) % RING) * inner_step + by * half
                            pltpu.make_async_copy(parts[kind][i].at[q, shift_x, shift_c], left.at[slot, pl.ds(pl.multiple_of(at, half), half)], arrive.at[slot]).start()

        def out_copy(t, slot):
            return pltpu.make_async_copy(left.at[slot, pl.ds(0, width)], cols_hbm.at[t], leave.at[slot])

        for slot in range(2):
            left[slot, width:, :] = jnp.zeros((16, frames), jnp.bfloat16)
        fetch(0, 0)

        def one(t, carry):
            slot = t % 2

            @pl.when(jnp.logical_and(t >= 1, t + 1 < tm_count))
            def _():
                out_copy(t - 1, 1 - slot).wait()

            @pl.when(t + 1 < tm_count)
            def _():
                fetch(t + 1, 1 - slot)

            pltpu.make_async_copy(cols_hbm.at[0], left.at[slot, pl.ds(0, width)], arrive.at[slot]).wait()
            left[slot, width:width + quarter, :] = rows_ref[t]
            out_copy(t, slot).start()
            part = lax.dot_general(left[slot], left[slot, :width, :], NT, preferred_element_type=jnp.float32)

            @pl.when(t == 0)
            def _():
                acc[...] = part

            @pl.when(t > 0)
            def _():
                acc[...] += part

            return carry

        lax.fori_loop(0, tm_count, one, 0)
        rows = lax.broadcasted_iota(jnp.int32, (NB, width), 0)
        cols = lax.broadcasted_iota(jnp.int32, (NB, width), 1)
        for at in range(0, width, NB):
            acc[at:at + NB, :] = acc[at:at + NB, :] * scale + jnp.where(rows + at == cols, noise_ref[...], 0.0)
            pltpu.make_async_copy(acc.at[pl.ds(at, NB)], gram_hbm.at[pl.ds(at, NB)], gram_sem).start()
        second = acc[width:width + quarter, :] * scale
        for i in range(group):
            second_ref[i] = second
        pltpu.make_async_copy(acc.at[pl.ds(0, width)], gram_hbm, gram_sem).wait()
        out_copy(tm_count - 2, 0).wait()
        out_copy(tm_count - 1, 1).wait()

    anywhere = pl.BlockSpec(memory_space=pl.ANY)
    return pl.pallas_call(
        kernel,
        out_shape=(pltpu.HBM((tm_count, width, frames), jnp.bfloat16), pltpu.HBM((width, width), jnp.float32),
                   jax.ShapeDtypeStruct((group, quarter, width), jnp.float32)),
        in_specs=[SCALARS] + [anywhere] * (2 * RING) + [WHOLE] * 2,
        out_specs=(HBM, HBM, WHOLE),
        scratch_shapes=[pltpu.VMEM((2, width + 16, frames), jnp.bfloat16), pltpu.VMEM((width + 16, width), jnp.float32),
                        pltpu.SemaphoreType.DMA((2,)), pltpu.SemaphoreType.DMA((2,)), pltpu.SemaphoreType.DMA],
        compiler_params=params(40), name="lead_gram")(place, *own, *other, second_rows, noise)


def two(z):
    high = z.astype(jnp.bfloat16)
    return high, (z - high.astype(jnp.float32)).astype(jnp.bfloat16)


def dot3(left, right):
    dot = lambda p, q: lax.dot_general(p, q, NT, preferred_element_type=jnp.float32)
    return dot(left[0], right[0]) + (dot(left[0], right[1]) + dot(left[1], right[0]))


STRIPS = 4


def lower_dot3(left_refs, right_refs, put):
    n = right_refs[0].shape[0]
    step = n // STRIPS
    for s in range(STRIPS):
        rows, k = pl.ds(s * step, step), (s + 1) * step
        put(s * step, step, dot3([r[:, :k] for r in left_refs], [r[rows, :k] for r in right_refs]))


def finish(rows, cols, diag, mine, theirs, inverse, prior, tm_index):
    quarter, cycles, frames = rows[0].shape
    width = cols.shape[1]
    half = width // 2
    plane, group = mine.shape[:2]
    count = quarter * cycles
    scale = 1.0 / (RING * frames)

    def kernel(tm_ref, r0, r1, r2, r3, cols_ref, diag_ref, mine_hbm, theirs_hbm, inv_hbm, prior_hbm, panel_hbm, next_hbm,
               rows_v, acc, gh, gl, prior_v, pieces, inv_v, ih, il, g, sh, sl, sems, row_sems):
        k = pl.program_id(0)
        left = tm_ref[0] % 2 == 0
        fetches = [
            pltpu.make_async_copy(inv_hbm, inv_v, sems.at[0]), pltpu.make_async_copy(mine_hbm, pieces.at[0], sems.at[1]),
            pltpu.make_async_copy(theirs_hbm, pieces.at[1], sems.at[2]), pltpu.make_async_copy(prior_hbm, prior_v, sems.at[3]),
        ]

        @pl.when(k == 0)
        def _():
            for i, r in enumerate((r0, r1, r2, r3)):
                pltpu.make_async_copy(r, rows_v.at[i], row_sems.at[i]).start()
            for f in fetches:
                f.start()

        pltpu.make_async_copy(r0, rows_v.at[k], row_sems.at[k]).wait()
        part = lax.dot_general(rows_v[k].reshape(count, frames), cols_ref[0], NT, preferred_element_type=jnp.float32)

        @pl.when(k == 0)
        def _():
            acc[...] = part.reshape(acc.shape)

        @pl.when(k > 0)
        def _():
            acc[...] += part.reshape(acc.shape)

        @pl.when(k == RING - 1)
        def _():
            for f in fetches:
                f.wait()
            tril = lax.broadcasted_iota(jnp.int32, (width, width), 0) >= lax.broadcasted_iota(jnp.int32, (width, width), 1)
            ih[...], il[...] = two(jnp.where(tril, inv_v[...], 0.0))
            cycle = lax.broadcasted_iota(jnp.int32, (1, cycles, width), 1)
            gram = acc[...] * scale + jnp.where(cycle == 0, diag_ref[...], 0.0)
            gh[...], gl[...] = two(gram.reshape(count, width))

            def put(at, size, value):
                acc[:, :, at:at + size] = value.reshape(quarter, cycles, size)

            lower_dot3([gh, gl], [ih, il], put)
            send_panel = pltpu.make_async_copy(acc, panel_hbm, sems.at[4])
            send_panel.start()

            def place(zy, carry):
                for xc in range(group):
                    at = pl.multiple_of((xc // 2 % 2) * half + zy * (width // 32) + (xc // 4) * 16 + (xc % 2) * 8, 8)
                    u, v = pieces[0, zy, xc], pieces[1, zy, xc]
                    inv_v[pl.ds(at, 8), :half] = jnp.where(left, u, v)
                    inv_v[pl.ds(at, 8), half:] = jnp.where(left, v, u)
                return carry

            lax.fori_loop(0, plane, place, 0)
            g[0], g[1] = two(inv_v[...])

            def put_second(at, size, value):
                sh[:, at:at + size], sl[:, at:at + size] = two(value)

            lower_dot3([g.at[0], g.at[1]], [ih, il], put_second)
            gh[...], gl[...] = two(acc[...].reshape(count, width))
            step = width // STRIPS
            for s in range(STRIPS):
                cut = pl.ds(s * step, step)
                update = dot3([gh[...], gl[...]], [sh[cut, :], sl[cut, :]])
                prior_v[:, :, s * step:(s + 1) * step] = prior_v[:, :, s * step:(s + 1) * step] - update.reshape(quarter, cycles, step)
            send_next = pltpu.make_async_copy(prior_v, next_hbm, sems.at[5])
            send_next.start()
            send_panel.wait()
            send_next.wait()

    out = jax.ShapeDtypeStruct((quarter, cycles, width), jnp.float32)
    square = pltpu.VMEM((width, width), jnp.bfloat16)
    return pl.pallas_call(
        kernel,
        out_shape=(out, out),
        grid_spec=pltpu.PrefetchScalarGridSpec(
            num_scalar_prefetch=1, grid=(RING,),
            in_specs=[HBM] * RING + [pl.BlockSpec((1, width, frames), lambda i, tm: (jnp.bitwise_xor(tm[0], i), 0, 0)),
                      pl.BlockSpec((quarter, 1, width), lambda i, tm: (0, 0, 0))] + [HBM] * 4,
            out_specs=(HBM, HBM),
            scratch_shapes=[pltpu.VMEM((RING, quarter, cycles, frames), jnp.bfloat16), pltpu.VMEM((quarter, cycles, width), jnp.float32)]
            + [pltpu.VMEM((count, width), jnp.bfloat16)] * 2
            + [pltpu.VMEM((quarter, cycles, width), jnp.float32), pltpu.VMEM((2,) + mine.shape, jnp.float32), pltpu.VMEM((width, width), jnp.float32)]
            + [square] * 2 + [pltpu.VMEM((2, width, width), jnp.bfloat16)] + [square] * 2
            + [pltpu.SemaphoreType.DMA((6,)), pltpu.SemaphoreType.DMA((RING,))]),
        compiler_params=params(56), name="finish")(tm_index, *map(in_hbm, rows), cols, diag, in_hbm(mine), in_hbm(theirs), in_hbm(inverse), in_hbm(prior))


def device_id(x, y, z, core):
    return ((x // 2) * 2 + core) * 32 + (x % 2) * 16 + z * 4 + y


DEVICES = [(x, y, z, c) for x in range(RING) for y in range(RING) for z in range(RING) for c in range(2)]


def send(value, step):
    return lax.ppermute(value, AXES, [(device_id(*d), device_id(*step(*d))) for d in DEVICES])


def swap_cores(value):
    return send(value, lambda x, y, z, c: (x, y, z, 1 - c))


def around(value, step):
    return [value] + [send(value, step(d)) for d in range(1, RING)]


def x_ring(d):
    return lambda x, y, z, c: ((x + d) % RING, y, z, c)


def inner_ring(d):
    return lambda x, y, z, c: (x, (y + d * (1 - c)) % RING, (z + d * c) % RING, c)


def outer_ring(d):
    return lambda x, y, z, c: (x, (y + d * c) % RING, (z + d * (1 - c)) % RING, c)


def flip_tm(k):
    return lambda x, y, z, c: (x ^ (k & 2), y, z, c ^ (k & 1))


CHIP_ROWS = [[device_id(x, y, z, c) for x in range(RING) for c in range(2)] for z in range(RING) for y in range(RING)]
PLANES = [[device_id(x, y, z, c) for z in range(RING) for y in range(RING)] for x in range(RING) for c in range(2)]


def shards(telemetry, frame_ids, valid, noise, prior_next):
    slope_index = lax.axis_index("slope")
    tm_index = lax.axis_index("tm")
    tel = telemetry[0]
    row_block, cycles, frames = tel.shape
    width = noise.shape[0]
    tm_count = 4
    quarter = row_block // tm_count
    core_index = tm_index % 2
    core = core_index.reshape(1)
    place = jnp.stack([core_index, (tm_index // 2) * 2 + slope_index // 16, slope_index % 4, (slope_index // 4) % 4])
    keep = lax.dynamic_slice(valid.reshape(cycles, 4), (0, slope_index // 8), (cycles, 1)).astype(jnp.float32)
    mine, theirs, second_own, hot = pick_first(tel, frame_ids[None, :], keep, core)
    pair = jnp.stack([mine, swap_cores(theirs)])
    by_x = jnp.stack(around(pair, x_ring))
    by_inner = jnp.stack(around(by_x, inner_ring))
    by_inner, hot, second_own = lax.optimization_barrier((by_inner, hot, second_own))
    own = around(by_inner, outer_ring)
    second_rows = lax.all_to_all(second_own.reshape(tm_count, quarter, frames), "tm", 0, 0)
    selected = pick_all(tel, hot, keep, tm_index.reshape(1))
    other = [swap_cores(piece) for piece in own]
    selected, own, other = lax.optimization_barrier((selected, own, other))
    rows = [selected[0], None, send(selected[2], flip_tm(2)), None]
    first_cols, lead, second_gram = lead_gram(own, other, second_rows, noise[None, :], place)
    near = lax.all_to_all(second_gram, AXES, 0, 0, axis_index_groups=CHIP_ROWS)
    big = chol_step(lead, 0, SPLIT[0])
    near, big, selected = lax.optimization_barrier((near, big, selected))
    rows[3] = send(selected[3], flip_tm(3))
    rows[1] = send(selected[1], flip_tm(1))
    near = lax.dynamic_slice_in_dim(near, core_index * (width // 2), width // 2, axis=2)
    near = jnp.broadcast_to(near[None], (16,) + near.shape)
    mine2 = lax.all_to_all(near, AXES, 0, 0, axis_index_groups=PLANES)
    big = chol_step(big, SPLIT[0], SPLIT[1])
    mine2, big = lax.optimization_barrier((mine2, big))
    theirs2 = swap_cores(mine2)
    big = chol_step(big, SPLIT[0] + SPLIT[1], SPLIT[2])
    diag_ids = slope_index * row_block + tm_index * quarter + lax.broadcasted_iota(jnp.int32, (quarter, 1, width), 0)
    diag = jnp.where(diag_ids == lax.broadcasted_iota(jnp.int32, (quarter, 1, width), 2), noise[None, None, :], 0.0)
    panel, next_block = finish(rows, first_cols, diag, mine2, theirs2, big, prior_next[0], tm_index.reshape(1))
    return panel[None], next_block[None]


def solution(mesh):
    return jax.shard_map(
        shards,
        mesh=mesh,
        in_specs=(P("slope", None, None, "tm"), P("tm"), P(), P(), P("slope", "tm", None, None)),
        out_specs=(P("slope", "tm", None, None), P("slope", "tm", None, None)),
        check_vma=False,
    )
```

```python
import jax
import jax.numpy as jnp
from jax import lax
from jax.experimental import pallas as pl
from jax.experimental.pallas import tpu as pltpu
from jax.sharding import PartitionSpec as P

NB = 128
MB = 8
TN = (((0,), (0,)), ((), ()))
NT = (((1,), (1,)), ((), ()))
WHOLE = pl.BlockSpec(memory_space=pltpu.VMEM)


def in_hbm(value):
    return pltpu.with_memory_space_constraint(value, pltpu.HBM)


def params(mib=40):
    return pltpu.CompilerParams(vmem_limit_bytes=mib * 2**20)


def bf16_round(z):
    return z.astype(jnp.bfloat16).astype(jnp.float32)


def split3(z):
    high = bf16_round(z)
    rest = z - high
    mid = bf16_round(rest)
    return high, mid, rest - mid


def row_of(z, j):
    return jnp.broadcast_to(z[j:j + 1, :], z.shape)


AHEAD = 2


def factor_block(wa, wx, out):
    sub = lax.broadcasted_iota(jnp.int32, (MB, NB), 0)
    groups = NB // MB
    rows_of = lambda k: (wa[k * MB:(k + 1) * MB, :], wx[k * MB:(k + 1) * MB, :])
    window = [rows_of(k) for k in range(AHEAD)]
    for k in range(groups):
        lo = MB * k
        if k + AHEAD < groups:
            window.append(rows_of(k + AHEAD))
        a, x = window.pop(0)
        columns = lambda z: [jnp.broadcast_to(z[:, lo + j:lo + j + 1], (MB, NB)) for j in range(MB)]
        cols = columns(a)
        others = [[na, nx, columns(na)] for na, nx in window]
        inv_d = jnp.zeros((MB, NB), jnp.float32)
        piv = jnp.zeros((MB, NB), jnp.float32)
        for j in range(MB):
            pivot = row_of(cols[j], j)
            recip = 1.0 / pivot
            mult = jnp.where(sub > j, cols[j] * recip, 0.0)
            ra, rx = row_of(a, j), row_of(x, j)
            rcs = {l: row_of(cols[l], j) for l in range(j + 1, MB)}
            for other in others:
                nmult = other[2][j] * recip
                other[0] = other[0] - nmult * ra
                other[1] = other[1] - nmult * rx
                for l in range(j + 1, MB):
                    other[2][l] = other[2][l] - nmult * rcs[l]
            for l in range(j + 1, MB):
                cols[l] = cols[l] - mult * rcs[l]
            a = a - mult * ra
            x = x - mult * rx
            inv_d = jnp.where(sub == j, recip, inv_d)
            piv = jnp.where(sub == j, pivot, piv)
        window = [(other[0], other[1]) for other in others]
        out[lo:lo + MB, :] = x * (1.0 / jnp.sqrt(piv))
        top = lo + (1 + AHEAD) * MB
        if top < NB:
            right = jnp.concatenate([a * inv_d, x * inv_d], axis=1)
            lh, lm, ll = split3(a)
            rh, rm, rl = split3(right)
            left_stack = jnp.concatenate([lh, lh, lm, lh, ll, lm], axis=0).astype(jnp.bfloat16)
            right_stack = jnp.concatenate([rh, rm, rh, rl, rh, rm], axis=0).astype(jnp.bfloat16)
            prod = lax.dot_general(left_stack, right_stack, TN, preferred_element_type=jnp.float32)
            wa[top:, :] = wa[top:, :] - prod[top:, :NB]
            wx[top:, :] = wx[top:, :] - prod[top:, NB:]


def chol_panels(first, count, src, dst, big, wa, wx, linv, ys, arrive, leave):
    n = big.shape[0]
    nblk = n // NB
    last = first + count - 1
    rows = lax.broadcasted_iota(jnp.int32, (NB, NB), 0)
    lanes = lax.broadcasted_iota(jnp.int32, (NB, NB), 1)
    eye = jnp.where(rows == lanes, 1.0, 0.0)

    def block(i):
        return pl.ds(pl.multiple_of(i * NB, NB), NB)

    def load(i):
        return pltpu.make_async_copy(src.at[block(i)], big.at[block(i)], arrive.at[i])

    def store(i):
        return pltpu.make_async_copy(big.at[block(i)], dst.at[block(i)], leave.at[i])

    for i in range(first, nblk):
        load(i).start()
    load(first).wait()

    def panel_step(p, carry):
        at = pl.multiple_of(p * NB, NB)
        wa[...] = big[pl.ds(at, NB), pl.ds(at, NB)]
        wx[...] = eye
        big[pl.ds(at, NB), pl.ds(at, NB)] = eye
        factor_block(wa, wx, linv)
        ih, im, il = (part.astype(jnp.bfloat16) for part in split3(linv[...]))
        rh, rm, rl = (part.astype(jnp.bfloat16) for part in split3(big[pl.ds(at, NB), :]))
        mul = lambda u, v: jnp.dot(jnp.concatenate(u, axis=1), jnp.concatenate(v, axis=0), preferred_element_type=jnp.float32)
        y = mul((ih, im), (rh, rm)) + (mul((im, ih), (rh, rm)) + mul((il, ih), (rh, rl)))
        big[pl.ds(at, NB), :] = y
        store(p).start()
        high, mid, low = (part.astype(jnp.bfloat16) for part in split3(y))
        for i, part in enumerate((high, mid, low, high)):
            ys[i * NB:(i + 1) * NB, :] = part

        def trail(u, c):
            row = pl.multiple_of(u * 2 * NB, 2 * NB)
            wide = pl.ds(row, 2 * NB)
            hm = ys[0:2 * NB, wide]
            mh = jnp.concatenate([ys[NB:2 * NB, wide], ys[0:NB, wide]], axis=0)
            lh = ys[2 * NB:4 * NB, wide]
            hl = jnp.concatenate([ys[0:NB, :], ys[2 * NB:3 * NB, :]], axis=0)
            dot = lambda u, v: lax.dot_general(u, v, TN, preferred_element_type=jnp.float32)
            upd = dot(hm, ys[0:2 * NB, :]) + (dot(mh, ys[0:2 * NB, :]) + dot(lh, hl))
            for h in range(2):
                i = 2 * u + h

                @pl.when(jnp.logical_and(i > p, p == first))
                def _():
                    load(i).wait()

                @pl.when(i > p)
                def _():
                    big[block(i), pl.ds(at, NB)] = jnp.zeros((NB, NB), jnp.float32)
                    big[block(i), :] = big[block(i), :] - upd[h * NB:(h + 1) * NB]

                @pl.when(jnp.logical_and(i > p, p == last))
                def _():
                    store(i).start()
            return c

        lax.fori_loop((p + 1) // 2, nblk // 2, trail, 0)
        return carry

    lax.fori_loop(first, last + 1, panel_step, 0)
    for i in range(first, nblk):
        store(i).wait()


CHOL_SCRATCH = [pltpu.VMEM((NB, NB), jnp.float32)] * 3


def chol_step(src, first, count):
    n = src.shape[0]
    blocks = n // NB

    def kernel(src_ref, dst_ref, big, wa, wx, linv, ys, arrive, leave):
        chol_panels(first, count, src_ref, dst_ref, big, wa, wx, linv, ys, arrive, leave)

    hbm = pl.BlockSpec(memory_space=pltpu.HBM)
    return pl.pallas_call(
        kernel, out_shape=pltpu.HBM((n, n), jnp.float32), in_specs=[hbm], out_specs=hbm,
        scratch_shapes=[pltpu.VMEM((n, n), jnp.float32)] + CHOL_SCRATCH
        + [pltpu.VMEM((4 * NB, n), jnp.bfloat16), pltpu.SemaphoreType.DMA((blocks,)), pltpu.SemaphoreType.DMA((blocks,))],
        input_output_aliases={0: 0}, compiler_params=params(24), name="chol_panels")(in_hbm(src))


SPLIT = (2, 5, 1)
AXES = ("tm", "slope")
RING = 4
SCALARS = pl.BlockSpec(memory_space=pltpu.SMEM)
HBM = pl.BlockSpec(memory_space=pltpu.HBM)


def pick_first(tel, ids, keep, core):
    rows, _, frames = tel.shape
    half = rows // 2

    def kernel(core_ref, tel_hbm, ids_ref, keep_ref, mine_ref, theirs_ref, second_ref, hot_ref, got, lead, tel_ref, sem):
        fetch = pltpu.make_async_copy(tel_hbm.at[:, pl.ds(0, 16), :], tel_ref, sem)
        fetch.start()
        hot_ref[...] = jnp.where(lax.broadcasted_iota(jnp.int32, (frames, frames), 0) == ids_ref[...], 1.0, 0.0).astype(jnp.bfloat16)
        fetch.wait()
        got[...] = tel_ref[...].astype(jnp.float32)
        both = jnp.concatenate([got[:, 0, :], got[:, 1, :]], axis=0).astype(jnp.bfloat16)
        both = jnp.dot(both, hot_ref[...], preferred_element_type=jnp.float32)
        lead[...] = both[:rows] * keep_ref[0:1, 0:1]
        at = pl.multiple_of(core_ref[0] * half, half)
        mine_ref[...] = lead[pl.ds(at, half), :].astype(jnp.bfloat16)
        theirs_ref[...] = lead[pl.ds(pl.multiple_of(half - at, half), half), :].astype(jnp.bfloat16)
        second_ref[...] = (both[rows:] * keep_ref[1:2, 0:1]).astype(jnp.bfloat16)

    whole = lambda shape: pl.BlockSpec(shape, lambda i: (0,) * len(shape))
    shapes = ((half, frames), (half, frames), (rows, frames), (frames, frames))
    return pl.pallas_call(
        kernel,
        grid=(1,),
        out_shape=tuple(jax.ShapeDtypeStruct(s, jnp.bfloat16) for s in shapes),
        in_specs=[SCALARS, HBM, whole((1, frames)), whole(keep.shape)],
        out_specs=tuple(whole(s) for s in shapes),
        scratch_shapes=[pltpu.VMEM((rows, 16, frames), jnp.float32), pltpu.VMEM((rows, frames), jnp.float32),
                        pltpu.VMEM((rows, 16, frames), tel.dtype), pltpu.SemaphoreType.DMA],
        compiler_params=params(), name="pick_first")(core, in_hbm(tel), ids, keep)


def pick_all(tel, hot, keep, tm_index):
    rows, cycles, frames = tel.shape
    per = 4
    quarter = rows // RING
    steps = quarter // per

    def kernel(tm_ref, tel_ref, hot_ref, keep_ref, *outs):
        got = jnp.dot(tel_ref[...].reshape(per * cycles, frames), hot_ref[...], preferred_element_type=jnp.float32)
        got = (got.reshape(per, cycles, frames) * keep_ref[...][None]).astype(jnp.bfloat16)
        for k in range(RING):
            @pl.when(pl.program_id(0) // steps == k)
            def _():
                outs[k][...] = got

    place = lambda k: pl.BlockSpec((per, cycles, frames), lambda i, tm: (jnp.clip(i - steps * k, 0, steps - 1), 0, 0))
    return pl.pallas_call(
        kernel, out_shape=(pltpu.HBM((quarter, cycles, frames), jnp.bfloat16),) * RING,
        grid_spec=pltpu.PrefetchScalarGridSpec(
            num_scalar_prefetch=1, grid=(rows // per,),
            in_specs=[pl.BlockSpec((per, cycles, frames), lambda i, tm: (jnp.bitwise_xor(tm[0], i // steps) * steps + i % steps, 0, 0)),
                      pl.BlockSpec((frames, frames), lambda i, tm: (0, 0)), pl.BlockSpec(keep.shape, lambda i, tm: (0, 0))],
            out_specs=tuple(place(k) for k in range(RING))),
        compiler_params=params(), name="pick_all")(tm_index, in_hbm(tel), hot, keep)


def lead_gram(own, other, second_rows, noise, place):
    width = noise.shape[1]
    tm_count, quarter, frames = second_rows.shape
    half = own[0].shape[3]
    scale = 1.0 / (tm_count * frames)
    group = 2 * RING
    extra = 16

    def kernel(place_ref, *refs):
        parts = (refs[:RING], refs[RING:2 * RING])
        rows_ref, noise_ref, cols_hbm, gram_hbm, second_ref, left, acc, arrive, leave, gram_sem = refs[2 * RING:]
        me_core, me_x, me_y, me_z = (place_ref[i] for i in range(4))

        def fetch(t, slot):
            x_hi, c = t // 2, t % 2
            for kind in range(2):
                by = me_core if kind == 0 else 1 - me_core
                on_z = by == 0
                outer_me, inner_me = jnp.where(on_z, me_z, me_y), jnp.where(on_z, me_y, me_z)
                outer_step, inner_step = jnp.where(on_z, width // 8, width // 32), jnp.where(on_z, width // 32, width // 8)
                shift_c = (by + c) % 2
                for x_lo in range(2):
                    shift_x = (me_x + RING - x_hi * 2 - x_lo) % RING
                    for i in range(RING):
                        for q in range(RING):
                            at = x_lo * (width // 2) + ((outer_me + RING - i) % RING) * outer_step + ((inner_me + RING - q) % RING) * inner_step + by * half
                            pltpu.make_async_copy(parts[kind][i].at[q, shift_x, shift_c], left.at[slot, pl.ds(pl.multiple_of(at + extra, half), half)], arrive.at[slot]).start()

        def out_copy(t, slot):
            return pltpu.make_async_copy(left.at[slot, pl.ds(extra, width)], cols_hbm.at[t], leave.at[slot])

        for slot in range(2):
            left[slot, :extra, :] = jnp.zeros((extra, frames), jnp.bfloat16)
        fetch(0, 0)

        def one(t, carry):
            slot = t % 2

            @pl.when(jnp.logical_and(t >= 1, t + 1 < tm_count))
            def _():
                out_copy(t - 1, 1 - slot).wait()

            @pl.when(t + 1 < tm_count)
            def _():
                fetch(t + 1, 1 - slot)

            pltpu.make_async_copy(cols_hbm.at[0], left.at[slot, pl.ds(extra, width)], arrive.at[slot]).wait()
            left[slot, :quarter, :] = rows_ref[t]
            out_copy(t, slot).start()
            strip = width // STRIPS
            for s in range(STRIPS):
                top, end = (extra + s * strip if s else 0), extra + (s + 1) * strip
                part = lax.dot_general(left[slot, top:end, :], left[slot, extra + s * strip:, :], NT, preferred_element_type=jnp.float32)

                @pl.when(t == 0)
                def _():
                    acc[top:end, s * strip:] = part

                @pl.when(t > 0)
                def _():
                    acc[top:end, s * strip:] += part
            return carry

        lax.fori_loop(0, tm_count, one, 0)
        rows = lax.broadcasted_iota(jnp.int32, (NB, width), 0)
        cols = lax.broadcasted_iota(jnp.int32, (NB, width), 1)
        for at in range(0, width, NB):
            cut = pl.ds(extra + at, NB)
            acc[cut, :] = acc[cut, :] * scale + jnp.where(rows + at == cols, noise_ref[...], 0.0)
            pltpu.make_async_copy(acc.at[cut], gram_hbm.at[pl.ds(at, NB)], gram_sem).start()
        second = acc[:quarter, :] * scale
        for i in range(group):
            second_ref[i] = second
        pltpu.make_async_copy(acc.at[pl.ds(extra, width)], gram_hbm, gram_sem).wait()
        out_copy(tm_count - 2, 0).wait()
        out_copy(tm_count - 1, 1).wait()

    anywhere = pl.BlockSpec(memory_space=pl.ANY)
    return pl.pallas_call(
        kernel,
        out_shape=(pltpu.HBM((tm_count, width, frames), jnp.bfloat16), pltpu.HBM((width, width), jnp.float32),
                   jax.ShapeDtypeStruct((group, quarter, width), jnp.float32)),
        in_specs=[SCALARS] + [anywhere] * (2 * RING) + [WHOLE] * 2,
        out_specs=(HBM, HBM, WHOLE),
        scratch_shapes=[pltpu.VMEM((2, width + extra, frames), jnp.bfloat16), pltpu.VMEM((width + extra, width), jnp.float32),
                        pltpu.SemaphoreType.DMA((2,)), pltpu.SemaphoreType.DMA((2,)), pltpu.SemaphoreType.DMA],
        compiler_params=params(40), name="lead_gram")(place, *own, *other, second_rows, noise)


def two(z):
    high = z.astype(jnp.bfloat16)
    return high, (z - high.astype(jnp.float32)).astype(jnp.bfloat16)


def dot3(left, right):
    dot = lambda p, q: lax.dot_general(p, q, NT, preferred_element_type=jnp.float32)
    return dot(left[0], right[0]) + (dot(left[0], right[1]) + dot(left[1], right[0]))


STRIPS = 4


def lower_dot3(left_refs, right_refs, put):
    n = right_refs[0].shape[0]
    step = n // STRIPS
    for s in range(STRIPS):
        rows, k = pl.ds(s * step, step), (s + 1) * step
        put(s * step, step, dot3([r[:, :k] for r in left_refs], [r[rows, :k] for r in right_refs]))


def finish(rows, cols, diag, mine, theirs, inverse, prior, tm_index):
    quarter, cycles, frames = rows[0].shape
    width = cols.shape[1]
    half = width // 2
    plane, group = mine.shape[:2]
    count = quarter * cycles
    scale = 1.0 / (RING * frames)

    def kernel(tm_ref, r0, r1, r2, r3, cols_ref, diag_ref, mine_hbm, theirs_hbm, inv_hbm, prior_hbm, panel_hbm, next_hbm,
               rows_v, acc, gh, gl, prior_v, pieces, inv_v, ih, il, g, sh, sl, sems, row_sems):
        k = pl.program_id(0)
        left = tm_ref[0] % 2 == 0
        fetches = [
            pltpu.make_async_copy(inv_hbm, inv_v, sems.at[0]), pltpu.make_async_copy(mine_hbm, pieces.at[0], sems.at[1]),
            pltpu.make_async_copy(theirs_hbm, pieces.at[1], sems.at[2]), pltpu.make_async_copy(prior_hbm, prior_v, sems.at[3]),
        ]

        @pl.when(k == 0)
        def _():
            for i, r in enumerate((r0, r1, r2, r3)):
                pltpu.make_async_copy(r, rows_v.at[i], row_sems.at[i]).start()
            for f in fetches:
                f.start()

        pltpu.make_async_copy(r0, rows_v.at[k], row_sems.at[k]).wait()
        part = lax.dot_general(rows_v[k].reshape(count, frames), cols_ref[0], NT, preferred_element_type=jnp.float32)

        @pl.when(k == 0)
        def _():
            acc[...] = part.reshape(acc.shape)

        @pl.when(k > 0)
        def _():
            acc[...] += part.reshape(acc.shape)

        @pl.when(k == RING - 1)
        def _():
            for f in fetches:
                f.wait()
            tril = lax.broadcasted_iota(jnp.int32, (width, width), 0) >= lax.broadcasted_iota(jnp.int32, (width, width), 1)
            ih[...], il[...] = two(jnp.where(tril, inv_v[...], 0.0))
            cycle = lax.broadcasted_iota(jnp.int32, (1, cycles, width), 1)
            gram = acc[...] * scale + jnp.where(cycle == 0, diag_ref[...], 0.0)
            gh[...], gl[...] = two(gram.reshape(count, width))

            def put(at, size, value):
                acc[:, :, at:at + size] = value.reshape(quarter, cycles, size)

            lower_dot3([gh, gl], [ih, il], put)
            send_panel = pltpu.make_async_copy(acc, panel_hbm, sems.at[4])
            send_panel.start()

            def place(zy, carry):
                for xc in range(group):
                    at = pl.multiple_of((xc // 2 % 2) * half + zy * (width // 32) + (xc // 4) * 16 + (xc % 2) * 8, 8)
                    u, v = pieces[0, zy, xc], pieces[1, zy, xc]
                    inv_v[pl.ds(at, 8), :half] = jnp.where(left, u, v)
                    inv_v[pl.ds(at, 8), half:] = jnp.where(left, v, u)
                return carry

            lax.fori_loop(0, plane, place, 0)
            g[0], g[1] = two(inv_v[...])

            def put_second(at, size, value):
                sh[:, at:at + size], sl[:, at:at + size] = two(value)

            lower_dot3([g.at[0], g.at[1]], [ih, il], put_second)
            gh[...], gl[...] = two(acc[...].reshape(count, width))
            step = width // STRIPS
            for s in range(STRIPS):
                cut = pl.ds(s * step, step)
                update = dot3([gh[...], gl[...]], [sh[cut, :], sl[cut, :]])
                prior_v[:, :, s * step:(s + 1) * step] = prior_v[:, :, s * step:(s + 1) * step] - update.reshape(quarter, cycles, step)
            send_next = pltpu.make_async_copy(prior_v, next_hbm, sems.at[5])
            send_next.start()
            send_panel.wait()
            send_next.wait()

    out = jax.ShapeDtypeStruct((quarter, cycles, width), jnp.float32)
    square = pltpu.VMEM((width, width), jnp.bfloat16)
    return pl.pallas_call(
        kernel,
        out_shape=(out, out),
        grid_spec=pltpu.PrefetchScalarGridSpec(
            num_scalar_prefetch=1, grid=(RING,),
            in_specs=[HBM] * RING + [pl.BlockSpec((1, width, frames), lambda i, tm: (jnp.bitwise_xor(tm[0], i), 0, 0)),
                      pl.BlockSpec((quarter, 1, width), lambda i, tm: (0, 0, 0))] + [HBM] * 4,
            out_specs=(HBM, HBM),
            scratch_shapes=[pltpu.VMEM((RING, quarter, cycles, frames), jnp.bfloat16), pltpu.VMEM((quarter, cycles, width), jnp.float32)]
            + [pltpu.VMEM((count, width), jnp.bfloat16)] * 2
            + [pltpu.VMEM((quarter, cycles, width), jnp.float32), pltpu.VMEM((2,) + mine.shape, jnp.float32), pltpu.VMEM((width, width), jnp.float32)]
            + [square] * 2 + [pltpu.VMEM((2, width, width), jnp.bfloat16)] + [square] * 2
            + [pltpu.SemaphoreType.DMA((6,)), pltpu.SemaphoreType.DMA((RING,))]),
        compiler_params=params(56), name="finish")(tm_index, *map(in_hbm, rows), cols, diag, in_hbm(mine), in_hbm(theirs), in_hbm(inverse), in_hbm(prior))


def device_id(x, y, z, core):
    return ((x // 2) * 2 + core) * 32 + (x % 2) * 16 + z * 4 + y


DEVICES = [(x, y, z, c) for x in range(RING) for y in range(RING) for z in range(RING) for c in range(2)]


def send(value, step):
    return lax.ppermute(value, AXES, [(device_id(*d), device_id(*step(*d))) for d in DEVICES])


def swap_cores(value):
    return send(value, lambda x, y, z, c: (x, y, z, 1 - c))


def around(value, step):
    return [value] + [send(value, step(d)) for d in range(1, RING)]


def x_ring(d):
    return lambda x, y, z, c: ((x + d) % RING, y, z, c)


def inner_ring(d):
    return lambda x, y, z, c: (x, (y + d * (1 - c)) % RING, (z + d * c) % RING, c)


def outer_ring(d):
    return lambda x, y, z, c: (x, (y + d * c) % RING, (z + d * (1 - c)) % RING, c)


def flip_tm(k):
    return lambda x, y, z, c: (x ^ (k & 2), y, z, c ^ (k & 1))


CHIP_ROWS = [[device_id(x, y, z, c) for x in range(RING) for c in range(2)] for z in range(RING) for y in range(RING)]
PLANES = [[device_id(x, y, z, c) for z in range(RING) for y in range(RING)] for x in range(RING) for c in range(2)]


def shards(telemetry, frame_ids, valid, noise, prior_next):
    slope_index = lax.axis_index("slope")
    tm_index = lax.axis_index("tm")
    tel = telemetry[0]
    row_block, cycles, frames = tel.shape
    width = noise.shape[0]
    tm_count = 4
    quarter = row_block // tm_count
    core_index = tm_index % 2
    core = core_index.reshape(1)
    place = jnp.stack([core_index, (tm_index // 2) * 2 + slope_index // 16, slope_index % 4, (slope_index // 4) % 4])
    keep = lax.dynamic_slice(valid.reshape(cycles, 4), (0, slope_index // 8), (cycles, 1)).astype(jnp.float32)
    mine, theirs, second_own, hot = pick_first(tel, frame_ids[None, :], keep, core)
    pair = jnp.stack([mine, swap_cores(theirs)])
    by_x = jnp.stack(around(pair, x_ring))
    by_inner = jnp.stack(around(by_x, inner_ring))
    by_inner, hot, second_own = lax.optimization_barrier((by_inner, hot, second_own))
    own = around(by_inner, outer_ring)
    second_rows = lax.all_to_all(second_own.reshape(tm_count, quarter, frames), "tm", 0, 0)
    selected = pick_all(tel, hot, keep, tm_index.reshape(1))
    other = [swap_cores(piece) for piece in own]
    selected, own, other = lax.optimization_barrier((selected, own, other))
    rows = [selected[0], None, send(selected[2], flip_tm(2)), None]
    first_cols, lead, second_gram = lead_gram(own, other, second_rows, noise[None, :], place)
    near = lax.all_to_all(second_gram, AXES, 0, 0, axis_index_groups=CHIP_ROWS)
    big = chol_step(lead, 0, SPLIT[0])
    near, big, selected = lax.optimization_barrier((near, big, selected))
    rows[3] = send(selected[3], flip_tm(3))
    rows[1] = send(selected[1], flip_tm(1))
    near = lax.dynamic_slice_in_dim(near, core_index * (width // 2), width // 2, axis=2)
    near = jnp.broadcast_to(near[None], (16,) + near.shape)
    mine2 = lax.all_to_all(near, AXES, 0, 0, axis_index_groups=PLANES)
    big = chol_step(big, SPLIT[0], SPLIT[1])
    mine2, big = lax.optimization_barrier((mine2, big))
    theirs2 = swap_cores(mine2)
    big = chol_step(big, SPLIT[0] + SPLIT[1], SPLIT[2])
    diag_ids = slope_index * row_block + tm_index * quarter + lax.broadcasted_iota(jnp.int32, (quarter, 1, width), 0)
    diag = jnp.where(diag_ids == lax.broadcasted_iota(jnp.int32, (quarter, 1, width), 2), noise[None, None, :], 0.0)
    panel, next_block = finish(rows, first_cols, diag, mine2, theirs2, big, prior_next[0], tm_index.reshape(1))
    return panel[None], next_block[None]


def solution(mesh):
    return jax.shard_map(
        shards,
        mesh=mesh,
        in_specs=(P("slope", None, None, "tm"), P("tm"), P(), P(), P("slope", "tm", None, None)),
        out_specs=(P("slope", "tm", None, None), P("slope", "tm", None, None)),
        check_vma=False,
    )
```

```python
import jax
import jax.numpy as jnp
from jax import lax
from jax.experimental import pallas as pl
from jax.experimental.pallas import tpu as pltpu
from jax.sharding import PartitionSpec as P

NB = 128
MB = 8
TN = (((0,), (0,)), ((), ()))
NT = (((1,), (1,)), ((), ()))
WHOLE = pl.BlockSpec(memory_space=pltpu.VMEM)


def in_hbm(value):
    return pltpu.with_memory_space_constraint(value, pltpu.HBM)


def params(mib=40):
    return pltpu.CompilerParams(vmem_limit_bytes=mib * 2**20)


def bf16_round(z):
    return z.astype(jnp.bfloat16).astype(jnp.float32)


def split3(z):
    high = bf16_round(z)
    rest = z - high
    mid = bf16_round(rest)
    return high, mid, rest - mid


def row_of(z, j):
    return jnp.broadcast_to(z[j:j + 1, :], z.shape)


AHEAD = 2


def factor_block(wa, wx, out):
    sub = lax.broadcasted_iota(jnp.int32, (MB, NB), 0)
    groups = NB // MB
    rows_of = lambda k: (wa[k * MB:(k + 1) * MB, :], wx[k * MB:(k + 1) * MB, :])
    window = [rows_of(k) for k in range(AHEAD)]
    for k in range(groups):
        lo = MB * k
        if k + AHEAD < groups:
            window.append(rows_of(k + AHEAD))
        a, x = window.pop(0)
        columns = lambda z: [jnp.broadcast_to(z[:, lo + j:lo + j + 1], (MB, NB)) for j in range(MB)]
        cols = columns(a)
        others = [[na, nx, columns(na)] for na, nx in window]
        inv_d = jnp.zeros((MB, NB), jnp.float32)
        piv = jnp.zeros((MB, NB), jnp.float32)
        for j in range(MB):
            pivot = row_of(cols[j], j)
            recip = 1.0 / pivot
            mult = jnp.where(sub > j, cols[j] * recip, 0.0)
            ra, rx = row_of(a, j), row_of(x, j)
            rcs = {l: row_of(cols[l], j) for l in range(j + 1, MB)}
            for other in others:
                nmult = other[2][j] * recip
                other[0] = other[0] - nmult * ra
                other[1] = other[1] - nmult * rx
                for l in range(j + 1, MB):
                    other[2][l] = other[2][l] - nmult * rcs[l]
            for l in range(j + 1, MB):
                cols[l] = cols[l] - mult * rcs[l]
            a = a - mult * ra
            x = x - mult * rx
            inv_d = jnp.where(sub == j, recip, inv_d)
            piv = jnp.where(sub == j, pivot, piv)
        window = [(other[0], other[1]) for other in others]
        out[lo:lo + MB, :] = x * (1.0 / jnp.sqrt(piv))
        top = lo + (1 + AHEAD) * MB
        if top < NB:
            right = jnp.concatenate([a * inv_d, x * inv_d], axis=1)
            lh, lm, ll = split3(a)
            rh, rm, rl = split3(right)
            left_stack = jnp.concatenate([lh, lh, lm, lh, ll, lm], axis=0).astype(jnp.bfloat16)
            right_stack = jnp.concatenate([rh, rm, rh, rl, rh, rm], axis=0).astype(jnp.bfloat16)
            prod = lax.dot_general(left_stack, right_stack, TN, preferred_element_type=jnp.float32)
            wa[top:, :] = wa[top:, :] - prod[top:, :NB]
            wx[top:, :] = wx[top:, :] - prod[top:, NB:]


def chol_panels(first, count, src, dst, big, wa, wx, linv, ys, arrive, leave):
    n = big.shape[0]
    nblk = n // NB
    last = first + count - 1
    rows = lax.broadcasted_iota(jnp.int32, (NB, NB), 0)
    lanes = lax.broadcasted_iota(jnp.int32, (NB, NB), 1)
    eye = jnp.where(rows == lanes, 1.0, 0.0)

    def block(i):
        return pl.ds(pl.multiple_of(i * NB, NB), NB)

    def load(i):
        return pltpu.make_async_copy(src.at[block(i)], big.at[block(i)], arrive.at[i])

    def store(i):
        return pltpu.make_async_copy(big.at[block(i)], dst.at[block(i)], leave.at[i])

    for i in range(first, nblk):
        load(i).start()
    load(first).wait()

    def panel_step(p, carry):
        at = pl.multiple_of(p * NB, NB)
        wa[...] = big[pl.ds(at, NB), pl.ds(at, NB)]
        wx[...] = eye
        big[pl.ds(at, NB), pl.ds(at, NB)] = eye
        factor_block(wa, wx, linv)
        ih, im, il = (part.astype(jnp.bfloat16) for part in split3(linv[...]))
        rh, rm, rl = (part.astype(jnp.bfloat16) for part in split3(big[pl.ds(at, NB), :]))
        mul = lambda u, v: jnp.dot(jnp.concatenate(u, axis=1), jnp.concatenate(v, axis=0), preferred_element_type=jnp.float32)
        y = mul((ih, im), (rh, rm)) + (mul((im, ih), (rh, rm)) + mul((il, ih), (rh, rl)))
        big[pl.ds(at, NB), :] = y
        store(p).start()
        high, mid, low = (part.astype(jnp.bfloat16) for part in split3(y))
        for i, part in enumerate((high, mid, low, high)):
            ys[i * NB:(i + 1) * NB, :] = part

        def trail(u, c):
            row = pl.multiple_of(u * 2 * NB, 2 * NB)
            wide = pl.ds(row, 2 * NB)
            hm = ys[0:2 * NB, wide]
            mh = jnp.concatenate([ys[NB:2 * NB, wide], ys[0:NB, wide]], axis=0)
            lh = ys[2 * NB:4 * NB, wide]
            hl = jnp.concatenate([ys[0:NB, :], ys[2 * NB:3 * NB, :]], axis=0)
            dot = lambda u, v: lax.dot_general(u, v, TN, preferred_element_type=jnp.float32)
            upd = dot(hm, ys[0:2 * NB, :]) + (dot(mh, ys[0:2 * NB, :]) + dot(lh, hl))
            for h in range(2):
                i = 2 * u + h

                @pl.when(jnp.logical_and(i > p, p == first))
                def _():
                    load(i).wait()

                @pl.when(i > p)
                def _():
                    big[block(i), pl.ds(at, NB)] = jnp.zeros((NB, NB), jnp.float32)
                    big[block(i), :] = big[block(i), :] - upd[h * NB:(h + 1) * NB]

                @pl.when(jnp.logical_and(i > p, p == last))
                def _():
                    store(i).start()
            return c

        lax.fori_loop((p + 1) // 2, nblk // 2, trail, 0)
        return carry

    lax.fori_loop(first, last + 1, panel_step, 0)
    for i in range(first, nblk):
        store(i).wait()


CHOL_SCRATCH = [pltpu.VMEM((NB, NB), jnp.float32)] * 3


def chol_step(src, first, count):
    n = src.shape[0]
    blocks = n // NB

    def kernel(src_ref, dst_ref, big, wa, wx, linv, ys, arrive, leave):
        chol_panels(first, count, src_ref, dst_ref, big, wa, wx, linv, ys, arrive, leave)

    hbm = pl.BlockSpec(memory_space=pltpu.HBM)
    return pl.pallas_call(
        kernel, out_shape=pltpu.HBM((n, n), jnp.float32), in_specs=[hbm], out_specs=hbm,
        scratch_shapes=[pltpu.VMEM((n, n), jnp.float32)] + CHOL_SCRATCH
        + [pltpu.VMEM((4 * NB, n), jnp.bfloat16), pltpu.SemaphoreType.DMA((blocks,)), pltpu.SemaphoreType.DMA((blocks,))],
        input_output_aliases={0: 0}, compiler_params=params(24), name="chol_panels")(in_hbm(src))


SPLIT = (2, 5, 1)
AXES = ("tm", "slope")
RING = 4
SCALARS = pl.BlockSpec(memory_space=pltpu.SMEM)
HBM = pl.BlockSpec(memory_space=pltpu.HBM)


def pick_first(tel, ids, valid, place):
    rows, _, frames = tel.shape
    half = rows // 2

    def kernel(place_ref, tel_hbm, ids_ref, valid_ref, mine_ref, theirs_ref, second_ref, hot_ref, got, lead, tel_ref, sem):
        fetch = pltpu.make_async_copy(tel_hbm.at[:, pl.ds(0, 16), :], tel_ref, sem)
        fetch.start()
        hot_ref[...] = jnp.where(lax.broadcasted_iota(jnp.int32, (frames, frames), 0) == ids_ref[...], 1.0, 0.0).astype(jnp.bfloat16)
        fetch.wait()
        got[...] = tel_ref[...].astype(jnp.float32)
        both = jnp.concatenate([got[:, 0, :], got[:, 1, :]], axis=0).astype(jnp.bfloat16)
        both = jnp.dot(both, hot_ref[...], preferred_element_type=jnp.float32)
        kept = [valid_ref[0, 4 * c + place_ref[1]].astype(jnp.float32) for c in range(2)]
        lead[...] = both[:rows] * kept[0]
        at = pl.multiple_of(place_ref[0] * half, half)
        mine_ref[...] = lead[pl.ds(at, half), :].astype(jnp.bfloat16)
        theirs_ref[...] = lead[pl.ds(pl.multiple_of(half - at, half), half), :].astype(jnp.bfloat16)
        second_ref[...] = (both[rows:] * kept[1]).astype(jnp.bfloat16)

    whole = lambda shape: pl.BlockSpec(shape, lambda i: (0,) * len(shape))
    shapes = ((half, frames), (half, frames), (rows, frames), (frames, frames))
    return pl.pallas_call(
        kernel,
        grid=(1,),
        out_shape=tuple(jax.ShapeDtypeStruct(s, jnp.bfloat16) for s in shapes),
        in_specs=[SCALARS, HBM, whole((1, frames)), SCALARS],
        out_specs=tuple(whole(s) for s in shapes),
        scratch_shapes=[pltpu.VMEM((rows, 16, frames), jnp.float32), pltpu.VMEM((rows, frames), jnp.float32),
                        pltpu.VMEM((rows, 16, frames), tel.dtype), pltpu.SemaphoreType.DMA],
        compiler_params=params(), name="pick_first")(place, in_hbm(tel), ids, valid)


def pick_all(tel, hot, keep, tm_index):
    rows, cycles, frames = tel.shape
    per = 4
    quarter = rows // RING
    steps = quarter // per

    def kernel(tm_ref, tel_ref, hot_ref, keep_ref, *outs):
        got = jnp.dot(tel_ref[...].reshape(per * cycles, frames), hot_ref[...], preferred_element_type=jnp.float32)
        got = (got.reshape(per, cycles, frames) * keep_ref[...][None]).astype(jnp.bfloat16)
        for k in range(RING):
            @pl.when(pl.program_id(0) // steps == k)
            def _():
                outs[k][...] = got

    place = lambda k: pl.BlockSpec((per, cycles, frames), lambda i, tm: (jnp.clip(i - steps * k, 0, steps - 1), 0, 0))
    return pl.pallas_call(
        kernel, out_shape=(pltpu.HBM((quarter, cycles, frames), jnp.bfloat16),) * RING,
        grid_spec=pltpu.PrefetchScalarGridSpec(
            num_scalar_prefetch=1, grid=(rows // per,),
            in_specs=[pl.BlockSpec((per, cycles, frames), lambda i, tm: (jnp.bitwise_xor(tm[0], i // steps) * steps + i % steps, 0, 0)),
                      pl.BlockSpec((frames, frames), lambda i, tm: (0, 0)), pl.BlockSpec(keep.shape, lambda i, tm: (0, 0))],
            out_specs=tuple(place(k) for k in range(RING))),
        compiler_params=params(), name="pick_all")(tm_index, in_hbm(tel), hot, keep)


def lead_gram(own, other, second_rows, noise, place):
    width = noise.shape[1]
    tm_count, quarter, frames = second_rows.shape
    half = own[0].shape[3]
    scale = 1.0 / (tm_count * frames)
    group = 2 * RING
    extra = 16

    def kernel(place_ref, *refs):
        parts = (refs[:RING], refs[RING:2 * RING])
        rows_ref, noise_ref, cols_hbm, gram_hbm, second_ref, left, acc, pieces, arrive, leave, gram_sem = refs[2 * RING:]
        me_core, me_x, me_y, me_z = (place_ref[i] for i in range(4))

        layout = []
        for kind in range(2):
            by = me_core if kind == 0 else 1 - me_core
            outer_me, inner_me = by * me_y + (1 - by) * me_z, by * me_z + (1 - by) * me_y
            outer_step, inner_step = (width // 8) * (1 - by) + (width // 32) * by, (width // 32) * (1 - by) + (width // 8) * by
            outer = [((outer_me - i) & (RING - 1)) * outer_step + by * half + extra for i in range(RING)]
            layout.append((by, outer, [((inner_me - q) & (RING - 1)) * inner_step for q in range(RING)]))

        def place(t, slot):
            x_hi, c = t >> 1, t & 1
            for kind in range(2):
                by, outer, inner = layout[kind]
                shift_c = (by + c) & 1
                for x_lo in range(2):
                    shift_x = (me_x - x_hi * 2 - x_lo) & (RING - 1)
                    for i in range(RING):
                        for q in range(RING):
                            at = pl.multiple_of(outer[i] + inner[q] + x_lo * (width // 2), half)
                            left[slot, pl.ds(at, half), :] = pieces[kind, i, q, shift_x, shift_c]

        def out_copy(t, slot):
            return pltpu.make_async_copy(left.at[slot, pl.ds(extra, width)], cols_hbm.at[t], leave.at[slot])

        for slot in range(2):
            left[slot, :extra, :] = jnp.zeros((extra, frames), jnp.bfloat16)
        loads = [pltpu.make_async_copy(parts[kind][i], pieces.at[kind, i], arrive.at[kind, i]) for kind in range(2) for i in range(RING)]
        for load in loads:
            load.start()
        for load in loads:
            load.wait()

        def one(t, carry):
            slot = t & 1

            @pl.when(t >= 2)
            def _():
                out_copy(t - 2, slot).wait()

            place(t, slot)
            left[slot, :quarter, :] = rows_ref[t]
            out_copy(t, slot).start()
            strip = width // STRIPS
            for s in range(STRIPS):
                top, end = (extra + s * strip if s else 0), extra + (s + 1) * strip
                part = lax.dot_general(left[slot, top:end, :], left[slot, extra + s * strip:, :], NT, preferred_element_type=jnp.float32)

                @pl.when(t == 0)
                def _():
                    acc[top:end, s * strip:] = part

                @pl.when(t > 0)
                def _():
                    acc[top:end, s * strip:] += part
            return carry

        lax.fori_loop(0, tm_count, one, 0)
        rows = lax.broadcasted_iota(jnp.int32, (NB, width), 0)
        cols = lax.broadcasted_iota(jnp.int32, (NB, width), 1)
        for at in range(0, width, NB):
            cut = pl.ds(extra + at, NB)
            acc[cut, :] = acc[cut, :] * scale + jnp.where(rows + at == cols, noise_ref[...], 0.0)
            pltpu.make_async_copy(acc.at[cut], gram_hbm.at[pl.ds(at, NB)], gram_sem).start()
        second = acc[:quarter, :] * scale
        for i in range(group):
            second_ref[i] = second
        pltpu.make_async_copy(acc.at[pl.ds(extra, width)], gram_hbm, gram_sem).wait()
        out_copy(tm_count - 2, 0).wait()
        out_copy(tm_count - 1, 1).wait()

    anywhere = pl.BlockSpec(memory_space=pl.ANY)
    return pl.pallas_call(
        kernel,
        out_shape=(pltpu.HBM((tm_count, width, frames), jnp.bfloat16), pltpu.HBM((width, width), jnp.float32),
                   jax.ShapeDtypeStruct((group, quarter, width), jnp.float32)),
        in_specs=[SCALARS] + [anywhere] * (2 * RING) + [WHOLE] * 2,
        out_specs=(HBM, HBM, WHOLE),
        scratch_shapes=[pltpu.VMEM((2, width + extra, frames), jnp.bfloat16), pltpu.VMEM((width + extra, width), jnp.float32),
                        pltpu.VMEM((2, RING) + own[0].shape, own[0].dtype), pltpu.SemaphoreType.DMA((2, RING)), pltpu.SemaphoreType.DMA((2,)), pltpu.SemaphoreType.DMA],
        compiler_params=params(40), name="lead_gram")(place, *own, *other, second_rows, noise)


def two(z):
    high = z.astype(jnp.bfloat16)
    return high, (z - high.astype(jnp.float32)).astype(jnp.bfloat16)


def dot3(left, right):
    dot = lambda p, q: lax.dot_general(p, q, NT, preferred_element_type=jnp.float32)
    return dot(left[0], right[0]) + (dot(left[0], right[1]) + dot(left[1], right[0]))


STRIPS = 4


def lower_dot3(left_refs, right_refs, put):
    n = right_refs[0].shape[0]
    step = n // STRIPS
    for s in range(STRIPS):
        rows, k = pl.ds(s * step, step), (s + 1) * step
        put(s * step, step, dot3([r[:, :k] for r in left_refs], [r[rows, :k] for r in right_refs]))


def finish(rows, cols, diag, mine, theirs, inverse, prior, tm_index):
    quarter, cycles, frames = rows[0].shape
    width = cols.shape[1]
    half = width // 2
    plane, group = mine.shape[:2]
    count = quarter * cycles
    scale = 1.0 / (RING * frames)

    def kernel(tm_ref, r0, r1, r2, r3, cols_ref, diag_ref, mine_hbm, theirs_hbm, inv_hbm, prior_hbm, panel_hbm, next_hbm,
               rows_v, acc, gh, gl, prior_v, pieces, inv_v, ih, il, g, sh, sl, sems, row_sems):
        k = pl.program_id(0)
        left = tm_ref[0] % 2 == 0
        fetches = [
            pltpu.make_async_copy(inv_hbm, inv_v, sems.at[0]), pltpu.make_async_copy(mine_hbm, pieces.at[0], sems.at[1]),
            pltpu.make_async_copy(theirs_hbm, pieces.at[1], sems.at[2]), pltpu.make_async_copy(prior_hbm, prior_v, sems.at[3]),
        ]

        @pl.when(k == 0)
        def _():
            for i, r in enumerate((r0, r1, r2, r3)):
                pltpu.make_async_copy(r, rows_v.at[i], row_sems.at[i]).start()
            for f in fetches:
                f.start()

        pltpu.make_async_copy(r0, rows_v.at[k], row_sems.at[k]).wait()
        part = lax.dot_general(rows_v[k].reshape(count, frames), cols_ref[0], NT, preferred_element_type=jnp.float32)

        @pl.when(k == 0)
        def _():
            acc[...] = part.reshape(acc.shape)

        @pl.when(k > 0)
        def _():
            acc[...] += part.reshape(acc.shape)

        @pl.when(k == RING - 1)
        def _():
            for f in fetches:
                f.wait()
            tril = lax.broadcasted_iota(jnp.int32, (width, width), 0) >= lax.broadcasted_iota(jnp.int32, (width, width), 1)
            ih[...], il[...] = two(jnp.where(tril, inv_v[...], 0.0))
            cycle = lax.broadcasted_iota(jnp.int32, (1, cycles, width), 1)
            gram = acc[...] * scale + jnp.where(cycle == 0, diag_ref[...], 0.0)
            gh[...], gl[...] = two(gram.reshape(count, width))

            def put(at, size, value):
                acc[:, :, at:at + size] = value.reshape(quarter, cycles, size)

            lower_dot3([gh, gl], [ih, il], put)
            send_panel = pltpu.make_async_copy(acc, panel_hbm, sems.at[4])
            send_panel.start()

            def place(zy, carry):
                for xc in range(group):
                    at = pl.multiple_of((xc // 2 % 2) * half + zy * (width // 32) + (xc // 4) * 16 + (xc % 2) * 8, 8)
                    u, v = pieces[0, zy, xc], pieces[1, zy, xc]
                    inv_v[pl.ds(at, 8), :half] = jnp.where(left, u, v)
                    inv_v[pl.ds(at, 8), half:] = jnp.where(left, v, u)
                return carry

            lax.fori_loop(0, plane, place, 0)
            g[0], g[1] = two(inv_v[...])

            def put_second(at, size, value):
                sh[:, at:at + size], sl[:, at:at + size] = two(value)

            lower_dot3([g.at[0], g.at[1]], [ih, il], put_second)
            gh[...], gl[...] = two(acc[...].reshape(count, width))
            step = width // STRIPS
            for s in range(STRIPS):
                cut = pl.ds(s * step, step)
                update = dot3([gh[...], gl[...]], [sh[cut, :], sl[cut, :]])
                prior_v[:, :, s * step:(s + 1) * step] = prior_v[:, :, s * step:(s + 1) * step] - update.reshape(quarter, cycles, step)
                part_of = lambda ref: ref.at[:, :, pl.ds(s * step, step)]
                pltpu.make_async_copy(part_of(prior_v), part_of(next_hbm), sems.at[5]).start()
            send_panel.wait()
            pltpu.make_async_copy(prior_v, next_hbm, sems.at[5]).wait()

    out = jax.ShapeDtypeStruct((quarter, cycles, width), jnp.float32)
    square = pltpu.VMEM((width, width), jnp.bfloat16)
    return pl.pallas_call(
        kernel,
        out_shape=(out, out),
        grid_spec=pltpu.PrefetchScalarGridSpec(
            num_scalar_prefetch=1, grid=(RING,),
            in_specs=[HBM] * RING + [pl.BlockSpec((1, width, frames), lambda i, tm: (jnp.bitwise_xor(tm[0], i), 0, 0)),
                      pl.BlockSpec((quarter, 1, width), lambda i, tm: (0, 0, 0))] + [HBM] * 4,
            out_specs=(HBM, HBM),
            scratch_shapes=[pltpu.VMEM((RING, quarter, cycles, frames), jnp.bfloat16), pltpu.VMEM((quarter, cycles, width), jnp.float32)]
            + [pltpu.VMEM((count, width), jnp.bfloat16)] * 2
            + [pltpu.VMEM((quarter, cycles, width), jnp.float32), pltpu.VMEM((2,) + mine.shape, jnp.float32), pltpu.VMEM((width, width), jnp.float32)]
            + [square] * 2 + [pltpu.VMEM((2, width, width), jnp.bfloat16)] + [square] * 2
            + [pltpu.SemaphoreType.DMA((6,)), pltpu.SemaphoreType.DMA((RING,))]),
        compiler_params=params(56), name="finish")(tm_index, *map(in_hbm, rows), cols, diag, in_hbm(mine), in_hbm(theirs), in_hbm(inverse), in_hbm(prior))


def device_id(x, y, z, core):
    return ((x // 2) * 2 + core) * 32 + (x % 2) * 16 + z * 4 + y


DEVICES = [(x, y, z, c) for x in range(RING) for y in range(RING) for z in range(RING) for c in range(2)]


def send(value, step):
    return lax.ppermute(value, AXES, [(device_id(*d), device_id(*step(*d))) for d in DEVICES])


def swap_cores(value):
    return send(value, lambda x, y, z, c: (x, y, z, 1 - c))


def around(value, step):
    return [value] + [send(value, step(d)) for d in range(1, RING)]


def x_ring(d):
    return lambda x, y, z, c: ((x + d) % RING, y, z, c)


def inner_ring(d):
    return lambda x, y, z, c: (x, (y + d * (1 - c)) % RING, (z + d * c) % RING, c)


def outer_ring(d):
    return lambda x, y, z, c: (x, (y + d * c) % RING, (z + d * (1 - c)) % RING, c)


def flip_tm(k):
    return lambda x, y, z, c: (x ^ (k & 2), y, z, c ^ (k & 1))


CHIP_ROWS = [[device_id(x, y, z, c) for x in range(RING) for c in range(2)] for z in range(RING) for y in range(RING)]
PLANES = [[device_id(x, y, z, c) for z in range(RING) for y in range(RING)] for x in range(RING) for c in range(2)]


def shards(telemetry, frame_ids, valid, noise, prior_next):
    slope_index = lax.axis_index("slope")
    tm_index = lax.axis_index("tm")
    tel = telemetry[0]
    row_block, cycles, frames = tel.shape
    width = noise.shape[0]
    tm_count = 4
    quarter = row_block // tm_count
    core_index = tm_index % 2
    place = jnp.stack([core_index, (tm_index // 2) * 2 + slope_index // 16, slope_index % 4, (slope_index // 4) % 4])
    keep = lax.dynamic_slice(valid.reshape(cycles, 4), (0, slope_index // 8), (cycles, 1)).astype(jnp.float32)
    mine, theirs, second_own, hot = pick_first(tel, frame_ids[None, :], valid, jnp.stack([core_index, slope_index // 8]))
    pair = jnp.stack([mine, swap_cores(theirs)])
    by_x = jnp.stack(around(pair, x_ring))
    by_inner = jnp.stack(around(by_x, inner_ring))
    by_inner, hot, second_own = lax.optimization_barrier((by_inner, hot, second_own))
    own = around(by_inner, outer_ring)
    second_rows = lax.all_to_all(second_own.reshape(tm_count, quarter, frames), "tm", 0, 0)
    selected = pick_all(tel, hot, keep, tm_index.reshape(1))
    rows = [selected[0], None, send(selected[2], flip_tm(2)), None]
    other = [swap_cores(piece) for piece in own]
    diag_ids = slope_index * row_block + tm_index * quarter + lax.broadcasted_iota(jnp.int32, (quarter, 1, width), 0)
    diag = jnp.where(diag_ids == lax.broadcasted_iota(jnp.int32, (quarter, 1, width), 2), noise[None, None, :], 0.0)
    selected, own, other, diag = lax.optimization_barrier((selected, own, other, diag))
    first_cols, lead, second_gram = lead_gram(own, other, second_rows, noise[None, :], place)
    near = lax.all_to_all(second_gram, AXES, 0, 0, axis_index_groups=CHIP_ROWS)
    big = chol_step(lead, 0, SPLIT[0])
    near, big, selected = lax.optimization_barrier((near, big, selected))
    rows[3] = send(selected[3], flip_tm(3))
    rows[1] = send(selected[1], flip_tm(1))
    near = lax.dynamic_slice_in_dim(near, core_index * (width // 2), width // 2, axis=2)
    near = jnp.broadcast_to(near[None], (16,) + near.shape)
    mine2 = lax.all_to_all(near, AXES, 0, 0, axis_index_groups=PLANES)
    big = chol_step(big, SPLIT[0], SPLIT[1])
    mine2, big = lax.optimization_barrier((mine2, big))
    theirs2 = swap_cores(mine2)
    big = chol_step(big, SPLIT[0] + SPLIT[1], SPLIT[2])
    panel, next_block = finish(rows, first_cols, diag, mine2, theirs2, big, prior_next[0], tm_index.reshape(1))
    return panel[None], next_block[None]


def solution(mesh):
    return jax.shard_map(
        shards,
        mesh=mesh,
        in_specs=(P("slope", None, None, "tm"), P("tm"), P(), P(), P("slope", "tm", None, None)),
        out_specs=(P("slope", "tm", None, None), P("slope", "tm", None, None)),
        check_vma=False,
    )
```

```python
import jax
import jax.numpy as jnp
from jax import lax
from jax.experimental import pallas as pl
from jax.experimental.pallas import tpu as pltpu
from jax.sharding import PartitionSpec as P

NB = 128
MB = 8
TN = (((0,), (0,)), ((), ()))
NT = (((1,), (1,)), ((), ()))
WHOLE = pl.BlockSpec(memory_space=pltpu.VMEM)


def in_hbm(value):
    return pltpu.with_memory_space_constraint(value, pltpu.HBM)


def params(mib=40):
    return pltpu.CompilerParams(vmem_limit_bytes=mib * 2**20)


def bf16_round(z):
    return z.astype(jnp.bfloat16).astype(jnp.float32)


def split3(z):
    high = bf16_round(z)
    rest = z - high
    mid = bf16_round(rest)
    return high, mid, rest - mid


def row_of(z, j):
    return jnp.broadcast_to(z[j:j + 1, :], z.shape)


AHEAD = 2


def factor_block(wa, wx, out):
    sub = lax.broadcasted_iota(jnp.int32, (MB, NB), 0)
    groups = NB // MB
    rows_of = lambda k: (wa[k * MB:(k + 1) * MB, :], wx[k * MB:(k + 1) * MB, :])
    window = [rows_of(k) for k in range(AHEAD)]
    for k in range(groups):
        lo = MB * k
        if k + AHEAD < groups:
            window.append(rows_of(k + AHEAD))
        a, x = window.pop(0)
        columns = lambda z: [jnp.broadcast_to(z[:, lo + j:lo + j + 1], (MB, NB)) for j in range(MB)]
        cols = columns(a)
        others = [[na, nx, columns(na)] for na, nx in window]
        inv_d = jnp.zeros((MB, NB), jnp.float32)
        piv = jnp.zeros((MB, NB), jnp.float32)
        for j in range(MB):
            pivot = row_of(cols[j], j)
            recip = 1.0 / pivot
            mult = jnp.where(sub > j, cols[j] * recip, 0.0)
            ra, rx = row_of(a, j), row_of(x, j)
            rcs = {l: row_of(cols[l], j) for l in range(j + 1, MB)}
            for other in others:
                nmult = other[2][j] * recip
                other[0] = other[0] - nmult * ra
                other[1] = other[1] - nmult * rx
                for l in range(j + 1, MB):
                    other[2][l] = other[2][l] - nmult * rcs[l]
            for l in range(j + 1, MB):
                cols[l] = cols[l] - mult * rcs[l]
            a = a - mult * ra
            x = x - mult * rx
            inv_d = jnp.where(sub == j, recip, inv_d)
            piv = jnp.where(sub == j, pivot, piv)
        window = [(other[0], other[1]) for other in others]
        out[lo:lo + MB, :] = x * (1.0 / jnp.sqrt(piv))
        top = lo + (1 + AHEAD) * MB
        if top < NB:
            right = jnp.concatenate([a * inv_d, x * inv_d], axis=1)
            lh, lm, ll = split3(a)
            rh, rm, rl = split3(right)
            left_stack = jnp.concatenate([lh, lh, lm, lh, ll, lm], axis=0).astype(jnp.bfloat16)
            right_stack = jnp.concatenate([rh, rm, rh, rl, rh, rm], axis=0).astype(jnp.bfloat16)
            prod = lax.dot_general(left_stack, right_stack, TN, preferred_element_type=jnp.float32)
            wa[top:, :] = wa[top:, :] - prod[top:, :NB]
            wx[top:, :] = wx[top:, :] - prod[top:, NB:]


def chol_panels(first, count, src, dst, big, wa, wx, linv, ys, arrive, leave):
    n = big.shape[0]
    nblk = n // NB
    last = first + count - 1
    rows = lax.broadcasted_iota(jnp.int32, (NB, NB), 0)
    lanes = lax.broadcasted_iota(jnp.int32, (NB, NB), 1)
    eye = jnp.where(rows == lanes, 1.0, 0.0)

    def block(i):
        return pl.ds(pl.multiple_of(i * NB, NB), NB)

    def load(i):
        return pltpu.make_async_copy(src.at[block(i)], big.at[block(i)], arrive.at[i])

    def store(i):
        return pltpu.make_async_copy(big.at[block(i)], dst.at[block(i)], leave.at[i])

    for i in range(first, nblk):
        load(i).start()
    load(first).wait()

    def panel_step(p, carry):
        at = pl.multiple_of(p * NB, NB)
        wa[...] = big[pl.ds(at, NB), pl.ds(at, NB)]
        wx[...] = eye
        big[pl.ds(at, NB), pl.ds(at, NB)] = eye
        factor_block(wa, wx, linv)
        ih, im, il = (part.astype(jnp.bfloat16) for part in split3(linv[...]))
        rh, rm, rl = (part.astype(jnp.bfloat16) for part in split3(big[pl.ds(at, NB), :]))
        mul = lambda u, v: jnp.dot(jnp.concatenate(u, axis=1), jnp.concatenate(v, axis=0), preferred_element_type=jnp.float32)
        y = mul((ih, im), (rh, rm)) + (mul((im, ih), (rh, rm)) + mul((il, ih), (rh, rl)))
        big[pl.ds(at, NB), :] = y
        store(p).start()
        high, mid, low = (part.astype(jnp.bfloat16) for part in split3(y))
        for i, part in enumerate((high, mid, low, high)):
            ys[i * NB:(i + 1) * NB, :] = part

        def trail(u, c):
            row = pl.multiple_of(u * 2 * NB, 2 * NB)
            wide = pl.ds(row, 2 * NB)
            hm = ys[0:2 * NB, wide]
            mh = jnp.concatenate([ys[NB:2 * NB, wide], ys[0:NB, wide]], axis=0)
            lh = ys[2 * NB:4 * NB, wide]
            hl = jnp.concatenate([ys[0:NB, :], ys[2 * NB:3 * NB, :]], axis=0)
            dot = lambda u, v: lax.dot_general(u, v, TN, preferred_element_type=jnp.float32)
            upd = dot(hm, ys[0:2 * NB, :]) + (dot(mh, ys[0:2 * NB, :]) + dot(lh, hl))
            for h in range(2):
                i = 2 * u + h

                @pl.when(jnp.logical_and(i > p, p == first))
                def _():
                    load(i).wait()

                @pl.when(i > p)
                def _():
                    big[block(i), pl.ds(at, NB)] = jnp.zeros((NB, NB), jnp.float32)
                    big[block(i), :] = big[block(i), :] - upd[h * NB:(h + 1) * NB]

                @pl.when(jnp.logical_and(i > p, p == last))
                def _():
                    store(i).start()
            return c

        lax.fori_loop((p + 1) // 2, nblk // 2, trail, 0)
        return carry

    lax.fori_loop(first, last + 1, panel_step, 0)
    for i in range(first, nblk):
        store(i).wait()


CHOL_SCRATCH = [pltpu.VMEM((NB, NB), jnp.float32)] * 3


def chol_step(src, first, count):
    n = src.shape[0]
    blocks = n // NB

    def kernel(src_ref, dst_ref, big, wa, wx, linv, ys, arrive, leave):
        chol_panels(first, count, src_ref, dst_ref, big, wa, wx, linv, ys, arrive, leave)

    hbm = pl.BlockSpec(memory_space=pltpu.HBM)
    return pl.pallas_call(
        kernel, out_shape=pltpu.HBM((n, n), jnp.float32), in_specs=[hbm], out_specs=hbm,
        scratch_shapes=[pltpu.VMEM((n, n), jnp.float32)] + CHOL_SCRATCH
        + [pltpu.VMEM((4 * NB, n), jnp.bfloat16), pltpu.SemaphoreType.DMA((blocks,)), pltpu.SemaphoreType.DMA((blocks,))],
        input_output_aliases={0: 0}, compiler_params=params(24), name="chol_panels")(in_hbm(src))


SPLIT = (1, 6, 1)
AXES = ("tm", "slope")
RING = 4
SCALARS = pl.BlockSpec(memory_space=pltpu.SMEM)
HBM = pl.BlockSpec(memory_space=pltpu.HBM)


def pick_first(tel, ids, keep, core):
    rows, _, frames = tel.shape
    half = rows // 2

    def kernel(core_ref, tel_hbm, ids_ref, keep_ref, mine_ref, theirs_ref, second_ref, hot_ref, got, lead, tel_ref, sem):
        fetch = pltpu.make_async_copy(tel_hbm.at[:, pl.ds(0, 16), :], tel_ref, sem)
        fetch.start()
        hot_ref[...] = jnp.where(lax.broadcasted_iota(jnp.int32, (frames, frames), 0) == ids_ref[...], 1.0, 0.0).astype(jnp.bfloat16)
        fetch.wait()
        got[...] = tel_ref[...].astype(jnp.float32)
        both = jnp.concatenate([got[:, 0, :], got[:, 1, :]], axis=0).astype(jnp.bfloat16)
        both = jnp.dot(both, hot_ref[...], preferred_element_type=jnp.float32)
        lead[...] = both[:rows] * keep_ref[0:1, 0:1]
        at = pl.multiple_of(core_ref[0] * half, half)
        mine_ref[...] = lead[pl.ds(at, half), :].astype(jnp.bfloat16)
        theirs_ref[...] = lead[pl.ds(pl.multiple_of(half - at, half), half), :].astype(jnp.bfloat16)
        second_ref[...] = (both[rows:] * keep_ref[1:2, 0:1]).astype(jnp.bfloat16)

    whole = lambda shape: pl.BlockSpec(shape, lambda i: (0,) * len(shape))
    shapes = ((half, frames), (half, frames), (rows, frames), (frames, frames))
    return pl.pallas_call(
        kernel,
        grid=(1,),
        out_shape=tuple(jax.ShapeDtypeStruct(s, jnp.bfloat16) for s in shapes),
        in_specs=[SCALARS, HBM, whole((1, frames)), whole(keep.shape)],
        out_specs=tuple(whole(s) for s in shapes),
        scratch_shapes=[pltpu.VMEM((rows, 16, frames), jnp.float32), pltpu.VMEM((rows, frames), jnp.float32),
                        pltpu.VMEM((rows, 16, frames), tel.dtype), pltpu.SemaphoreType.DMA],
        compiler_params=params(), name="pick_first")(core, in_hbm(tel), ids, keep)


def pick_all(tel, hot, keep, tm_index):
    rows, cycles, frames = tel.shape
    per = 4
    quarter = rows // RING
    steps = quarter // per

    def kernel(tm_ref, tel_ref, hot_ref, keep_ref, *outs):
        got = jnp.dot(tel_ref[...].reshape(per * cycles, frames), hot_ref[...], preferred_element_type=jnp.float32)
        got = (got.reshape(per, cycles, frames) * keep_ref[...][None]).astype(jnp.bfloat16)
        for k in range(RING):
            @pl.when(pl.program_id(0) // steps == k)
            def _():
                outs[k][...] = got

    place = lambda k: pl.BlockSpec((per, cycles, frames), lambda i, tm: (jnp.clip(i - steps * k, 0, steps - 1), 0, 0))
    return pl.pallas_call(
        kernel, out_shape=(pltpu.HBM((quarter, cycles, frames), jnp.bfloat16),) * RING,
        grid_spec=pltpu.PrefetchScalarGridSpec(
            num_scalar_prefetch=1, grid=(rows // per,),
            in_specs=[pl.BlockSpec((per, cycles, frames), lambda i, tm: (jnp.bitwise_xor(tm[0], i // steps) * steps + i % steps, 0, 0)),
                      pl.BlockSpec((frames, frames), lambda i, tm: (0, 0)), pl.BlockSpec(keep.shape, lambda i, tm: (0, 0))],
            out_specs=tuple(place(k) for k in range(RING))),
        compiler_params=params(), name="pick_all")(tm_index, in_hbm(tel), hot, keep)


def lead_gram(own, other, second_rows, noise, place):
    width = noise.shape[1]
    tm_count, quarter, frames = second_rows.shape
    half = own[0].shape[3]
    scale = 1.0 / (tm_count * frames)
    group = 2 * RING
    extra = 16

    def kernel(place_ref, *refs):
        parts = (refs[:RING], refs[RING:2 * RING])
        rows_ref, noise_ref, cols_hbm, gram_hbm, second_ref, left, acc, pieces, arrive, leave, gram_sem = refs[2 * RING:]
        me_core, me_x, me_y, me_z = (place_ref[i] for i in range(4))

        layout = []
        for kind in range(2):
            by = me_core if kind == 0 else 1 - me_core
            outer_me, inner_me = by * me_y + (1 - by) * me_z, by * me_z + (1 - by) * me_y
            outer_step, inner_step = (width // 8) * (1 - by) + (width // 32) * by, (width // 32) * (1 - by) + (width // 8) * by
            outer = [((outer_me - i) & (RING - 1)) * outer_step + by * half + extra for i in range(RING)]
            layout.append((by, outer, [((inner_me - q) & (RING - 1)) * inner_step for q in range(RING)]))

        def place(t, slot):
            x_hi, c = t >> 1, t & 1
            for kind in range(2):
                by, outer, inner = layout[kind]
                shift_c = (by + c) & 1
                for x_lo in range(2):
                    shift_x = (me_x - x_hi * 2 - x_lo) & (RING - 1)
                    for i in range(RING):
                        for q in range(RING):
                            at = pl.multiple_of(outer[i] + inner[q] + x_lo * (width // 2), half)
                            left[slot, pl.ds(at, half), :] = pieces[kind, i, q, shift_x, shift_c]

        def out_copy(t, slot):
            return pltpu.make_async_copy(left.at[slot, pl.ds(extra, width)], cols_hbm.at[t], leave.at[slot])

        for slot in range(2):
            left[slot, :extra, :] = jnp.zeros((extra, frames), jnp.bfloat16)
        loads = [pltpu.make_async_copy(parts[kind][i], pieces.at[kind, i], arrive.at[kind, i]) for kind in range(2) for i in range(RING)]
        for load in loads:
            load.start()
        for load in loads:
            load.wait()

        def one(t, carry):
            slot = t & 1

            @pl.when(t >= 2)
            def _():
                out_copy(t - 2, slot).wait()

            place(t, slot)
            left[slot, :quarter, :] = rows_ref[t]
            out_copy(t, slot).start()
            strip = width // STRIPS
            for s in range(STRIPS):
                top, end = (extra + s * strip if s else 0), extra + (s + 1) * strip
                part = lax.dot_general(left[slot, top:end, :], left[slot, extra + s * strip:, :], NT, preferred_element_type=jnp.float32)

                @pl.when(t == 0)
                def _():
                    acc[top:end, s * strip:] = part

                @pl.when(t > 0)
                def _():
                    acc[top:end, s * strip:] += part
            return carry

        lax.fori_loop(0, tm_count, one, 0)
        rows = lax.broadcasted_iota(jnp.int32, (NB, width), 0)
        cols = lax.broadcasted_iota(jnp.int32, (NB, width), 1)
        for at in range(0, width, NB):
            cut = pl.ds(extra + at, NB)
            acc[cut, :] = acc[cut, :] * scale + jnp.where(rows + at == cols, noise_ref[...], 0.0)
            pltpu.make_async_copy(acc.at[cut], gram_hbm.at[pl.ds(at, NB)], gram_sem).start()
        second = acc[:quarter, :] * scale
        for i in range(group):
            second_ref[i] = second
        pltpu.make_async_copy(acc.at[pl.ds(extra, width)], gram_hbm, gram_sem).wait()
        out_copy(tm_count - 2, 0).wait()
        out_copy(tm_count - 1, 1).wait()

    anywhere = pl.BlockSpec(memory_space=pl.ANY)
    return pl.pallas_call(
        kernel,
        out_shape=(pltpu.HBM((tm_count, width, frames), jnp.bfloat16), pltpu.HBM((width, width), jnp.float32),
                   jax.ShapeDtypeStruct((group, quarter, width), jnp.float32)),
        in_specs=[SCALARS] + [anywhere] * (2 * RING) + [WHOLE] * 2,
        out_specs=(HBM, HBM, WHOLE),
        scratch_shapes=[pltpu.VMEM((2, width + extra, frames), jnp.bfloat16), pltpu.VMEM((width + extra, width), jnp.float32),
                        pltpu.VMEM((2, RING) + own[0].shape, own[0].dtype), pltpu.SemaphoreType.DMA((2, RING)), pltpu.SemaphoreType.DMA((2,)), pltpu.SemaphoreType.DMA],
        compiler_params=params(40), name="lead_gram")(place, *own, *other, second_rows, noise)


def two(z):
    high = z.astype(jnp.bfloat16)
    return high, (z - high.astype(jnp.float32)).astype(jnp.bfloat16)


def dot3(left, right):
    dot = lambda p, q: lax.dot_general(p, q, NT, preferred_element_type=jnp.float32)
    return dot(left[0], right[0]) + (dot(left[0], right[1]) + dot(left[1], right[0]))


STRIPS = 4


def lower_dot3(left_refs, right_refs, put):
    n = right_refs[0].shape[0]
    step = n // STRIPS
    for s in range(STRIPS):
        rows, k = pl.ds(s * step, step), (s + 1) * step
        put(s * step, step, dot3([r[:, :k] for r in left_refs], [r[rows, :k] for r in right_refs]))


def finish(rows, cols, diag, mine, theirs, inverse, prior, tm_index):
    quarter, cycles, frames = rows[0].shape
    width = cols.shape[1]
    half = width // 2
    plane, group = mine.shape[:2]
    count = quarter * cycles
    scale = 1.0 / (RING * frames)

    def kernel(tm_ref, r0, r1, r2, r3, cols_ref, diag_ref, mine_hbm, theirs_hbm, inv_hbm, prior_hbm, panel_hbm, next_hbm,
               rows_v, acc, gh, gl, prior_v, pieces, inv_v, ih, il, g, sh, sl, sems, row_sems):
        k = pl.program_id(0)
        left = tm_ref[0] % 2 == 0
        fetches = [
            pltpu.make_async_copy(inv_hbm, inv_v, sems.at[0]), pltpu.make_async_copy(mine_hbm, pieces.at[0], sems.at[1]),
            pltpu.make_async_copy(theirs_hbm, pieces.at[1], sems.at[2]), pltpu.make_async_copy(prior_hbm, prior_v, sems.at[3]),
        ]

        @pl.when(k == 0)
        def _():
            for i, r in enumerate((r0, r1, r2, r3)):
                pltpu.make_async_copy(r, rows_v.at[i], row_sems.at[i]).start()
            for f in fetches:
                f.start()

        pltpu.make_async_copy(r0, rows_v.at[k], row_sems.at[k]).wait()
        part = lax.dot_general(rows_v[k].reshape(count, frames), cols_ref[0], NT, preferred_element_type=jnp.float32)

        @pl.when(k == 0)
        def _():
            acc[...] = part.reshape(acc.shape)

        @pl.when(k > 0)
        def _():
            acc[...] += part.reshape(acc.shape)

        @pl.when(k == RING - 1)
        def _():
            for f in fetches:
                f.wait()
            tril = lax.broadcasted_iota(jnp.int32, (width, width), 0) >= lax.broadcasted_iota(jnp.int32, (width, width), 1)
            ih[...], il[...] = two(jnp.where(tril, inv_v[...], 0.0))
            cycle = lax.broadcasted_iota(jnp.int32, (1, cycles, width), 1)
            gram = acc[...] * scale + jnp.where(cycle == 0, diag_ref[...], 0.0)
            gh[...], gl[...] = two(gram.reshape(count, width))

            def put(at, size, value):
                acc[:, :, at:at + size] = value.reshape(quarter, cycles, size)

            lower_dot3([gh, gl], [ih, il], put)
            send_panel = pltpu.make_async_copy(acc, panel_hbm, sems.at[4])
            send_panel.start()

            def place(zy, carry):
                for xc in range(group):
                    at = pl.multiple_of((xc // 2 % 2) * half + zy * (width // 32) + (xc // 4) * 16 + (xc % 2) * 8, 8)
                    u, v = pieces[0, zy, xc], pieces[1, zy, xc]
                    inv_v[pl.ds(at, 8), :half] = jnp.where(left, u, v)
                    inv_v[pl.ds(at, 8), half:] = jnp.where(left, v, u)
                return carry

            lax.fori_loop(0, plane, place, 0)
            g[0], g[1] = two(inv_v[...])

            def put_second(at, size, value):
                sh[:, at:at + size], sl[:, at:at + size] = two(value)

            lower_dot3([g.at[0], g.at[1]], [ih, il], put_second)
            gh[...], gl[...] = two(acc[...].reshape(count, width))
            step = width // STRIPS
            for s in range(STRIPS):
                cut = pl.ds(s * step, step)
                update = dot3([gh[...], gl[...]], [sh[cut, :], sl[cut, :]])
                prior_v[:, :, s * step:(s + 1) * step] = prior_v[:, :, s * step:(s + 1) * step] - update.reshape(quarter, cycles, step)
                part_of = lambda ref: ref.at[:, :, pl.ds(s * step, step)]
                pltpu.make_async_copy(part_of(prior_v), part_of(next_hbm), sems.at[5]).start()
            send_panel.wait()
            pltpu.make_async_copy(prior_v, next_hbm, sems.at[5]).wait()

    out = jax.ShapeDtypeStruct((quarter, cycles, width), jnp.float32)
    square = pltpu.VMEM((width, width), jnp.bfloat16)
    return pl.pallas_call(
        kernel,
        out_shape=(out, out),
        grid_spec=pltpu.PrefetchScalarGridSpec(
            num_scalar_prefetch=1, grid=(RING,),
            in_specs=[HBM] * RING + [pl.BlockSpec((1, width, frames), lambda i, tm: (jnp.bitwise_xor(tm[0], i), 0, 0)),
                      pl.BlockSpec((quarter, 1, width), lambda i, tm: (0, 0, 0))] + [HBM] * 4,
            out_specs=(HBM, HBM),
            scratch_shapes=[pltpu.VMEM((RING, quarter, cycles, frames), jnp.bfloat16), pltpu.VMEM((quarter, cycles, width), jnp.float32)]
            + [pltpu.VMEM((count, width), jnp.bfloat16)] * 2
            + [pltpu.VMEM((quarter, cycles, width), jnp.float32), pltpu.VMEM((2,) + mine.shape, jnp.float32), pltpu.VMEM((width, width), jnp.float32)]
            + [square] * 2 + [pltpu.VMEM((2, width, width), jnp.bfloat16)] + [square] * 2
            + [pltpu.SemaphoreType.DMA((6,)), pltpu.SemaphoreType.DMA((RING,))]),
        compiler_params=params(56), name="finish")(tm_index, *map(in_hbm, rows), cols, diag, in_hbm(mine), in_hbm(theirs), in_hbm(inverse), in_hbm(prior))


def device_id(x, y, z, core):
    return ((x // 2) * 2 + core) * 32 + (x % 2) * 16 + z * 4 + y


DEVICES = [(x, y, z, c) for x in range(RING) for y in range(RING) for z in range(RING) for c in range(2)]


def send(value, step):
    return lax.ppermute(value, AXES, [(device_id(*d), device_id(*step(*d))) for d in DEVICES])


def swap_cores(value):
    return send(value, lambda x, y, z, c: (x, y, z, 1 - c))


def around(value, step):
    return [value] + [send(value, step(d)) for d in range(1, RING)]


def x_ring(d):
    return lambda x, y, z, c: ((x + d) % RING, y, z, c)


def inner_ring(d):
    return lambda x, y, z, c: (x, (y + d * (1 - c)) % RING, (z + d * c) % RING, c)


def outer_ring(d):
    return lambda x, y, z, c: (x, (y + d * c) % RING, (z + d * (1 - c)) % RING, c)


def flip_tm(k):
    return lambda x, y, z, c: (x ^ (k & 2), y, z, c ^ (k & 1))


CHIP_ROWS = [[device_id(x, y, z, c) for x in range(RING) for c in range(2)] for z in range(RING) for y in range(RING)]
PLANES = [[device_id(x, y, z, c) for z in range(RING) for y in range(RING)] for x in range(RING) for c in range(2)]


def shards(telemetry, frame_ids, valid, noise, prior_next):
    slope_index = lax.axis_index("slope")
    tm_index = lax.axis_index("tm")
    tel = telemetry[0]
    row_block, cycles, frames = tel.shape
    width = noise.shape[0]
    tm_count = 4
    quarter = row_block // tm_count
    core_index = tm_index % 2
    core = core_index.reshape(1)
    place = jnp.stack([core_index, (tm_index // 2) * 2 + slope_index // 16, slope_index % 4, (slope_index // 4) % 4])
    keep = lax.dynamic_slice(valid.reshape(cycles, 4), (0, slope_index // 8), (cycles, 1)).astype(jnp.float32)
    mine, theirs, second_own, hot = pick_first(tel, frame_ids[None, :], keep, core)
    pair = jnp.stack([mine, swap_cores(theirs)])
    by_x = jnp.stack(around(pair, x_ring))
    by_inner = jnp.stack(around(by_x, inner_ring))
    by_inner, hot, second_own = lax.optimization_barrier((by_inner, hot, second_own))
    own = around(by_inner, outer_ring)
    second_rows = lax.all_to_all(second_own.reshape(tm_count, quarter, frames), "tm", 0, 0)
    selected = pick_all(tel, hot, keep, tm_index.reshape(1))
    rows = [selected[0], None, send(selected[2], flip_tm(2)), None]
    other = [swap_cores(piece) for piece in own]
    selected, own, other = lax.optimization_barrier((selected, own, other))
    first_cols, lead, second_gram = lead_gram(own, other, second_rows, noise[None, :], place)
    near = lax.all_to_all(second_gram, AXES, 0, 0, axis_index_groups=CHIP_ROWS)
    big = chol_step(lead, 0, SPLIT[0])
    near, big, selected = lax.optimization_barrier((near, big, selected))
    rows[3] = send(selected[3], flip_tm(3))
    rows[1] = send(selected[1], flip_tm(1))
    near = lax.dynamic_slice_in_dim(near, core_index * (width // 2), width // 2, axis=2)
    near = jnp.broadcast_to(near[None], (16,) + near.shape)
    mine2 = lax.all_to_all(near, AXES, 0, 0, axis_index_groups=PLANES)
    big = chol_step(big, SPLIT[0], SPLIT[1])
    mine2, big = lax.optimization_barrier((mine2, big))
    theirs2 = swap_cores(mine2)
    big = chol_step(big, SPLIT[0] + SPLIT[1], SPLIT[2])
    diag_ids = slope_index * row_block + tm_index * quarter + lax.broadcasted_iota(jnp.int32, (quarter, 1, width), 0)
    diag = jnp.where(diag_ids == lax.broadcasted_iota(jnp.int32, (quarter, 1, width), 2), noise[None, None, :], 0.0)
    panel, next_block = finish(rows, first_cols, diag, mine2, theirs2, big, prior_next[0], tm_index.reshape(1))
    return panel[None], next_block[None]


def solution(mesh):
    return jax.shard_map(
        shards,
        mesh=mesh,
        in_specs=(P("slope", None, None, "tm"), P("tm"), P(), P(), P("slope", "tm", None, None)),
        out_specs=(P("slope", "tm", None, None), P("slope", "tm", None, None)),
        check_vma=False,
    )
```
